32 devices in a mesh: pipe: 4 (over y, core), dp: 4 (over z), head: 2 (over x).
Axes of the slice: x: 2, y: 2, z: 4, core: 2. Of those that a mesh axis runs over, the one named last changes fastest.
Arguments:
- activations: bfloat16 [4, 2, 896, 8192], P('pipe', None, 'dp', 'head'), may hold values from -6 to 6
- out_grad: bfloat16 [4, 896, 8192], P('pipe', 'dp', 'head'), may hold values from -1.5 to 1.5
- key_grad: bfloat16 [4, 2, 896, 512], P('pipe', None, 'dp', 'head'), may hold values from -1.5 to 1.5
- key_weight: bfloat16 [4, 8192, 512], P('pipe', 'head'), may hold values from -0.25 to 0.25
- plan: int32 [4, 2], P('pipe'), may hold values from 0 to 1, each once within a row
- first_moment: bfloat16 [4, 2, 4096, 512], P('pipe', 'head', 'dp'), may hold values from -48 to 48
- second_moment: bfloat16 [4, 2, 4096, 512], P('pipe', 'head', 'dp'), may hold values from 10 to 300
Outputs:
- received_grad: bfloat16 [4, 896, 8192], P('pipe', 'dp', 'head')
- new_weight: bfloat16 [4, 2, 4096, 512], P('pipe', 'head', 'dp')
- new_first_moment: bfloat16 [4, 2, 4096, 512], P('pipe', 'head', 'dp')
- new_second_moment: bfloat16 [4, 2, 4096, 512], P('pipe', 'head', 'dp')
- checksum: float32 [4, 2, 4, 512], P('pipe', 'head', 'dp')
The draws below stay inside these ranges and needn't reach their ends.
Inputs may be any that keep to these rules, and one draw needn't show every extreme that they name: Each row of plan holds 0 and 1 once each.
All inputs are finite; a program needn't handle non-finite values.
Results may differ from the reference program's by a relative error of at most 0.0043.
Values may be sent and summed in bfloat16 or wider, within the bound.
No kernel may reach another device: no remote copies, remote signals or barrier semaphores. Data moves between devices by JAX's collectives and lax.ppermute only.
A program may use at most 64 MiB of HBM per device.

```python
import math
import jax
import jax.numpy as jnp
from jax import lax

D = 8192
SECTIONS = 4
TOKENS = 896
KV_COLS = 512
GROUPS = 2
FEAT = 4096
N_DP = 4


def block_scale(rng, shape, pieces, smallest, largest):
    loudness = 1.0
    for dim, blocks in pieces:
        draws = jax.random.uniform(jax.random.fold_in(jax.random.fold_in(rng, 6), dim), (blocks,), jnp.float32, smallest / len(pieces), largest / len(pieces))
        loudness = loudness * jnp.repeat(jnp.exp(draws), shape[dim] // blocks).reshape((-1,) + (1,) * (len(shape) - 1 - dim))
    return loudness


def noise(rng, extent, deviation, bound, split=(), kind=jnp.bfloat16):
    array = jax.random.normal(rng, extent, jnp.float32) * deviation
    if len(split) > 0:
        array = block_scale(rng, extent, split, -0.22, 0.18) * array
    return jnp.clip(array, min=-bound, max=bound).astype(kind)


def setup_inputs(seed: int = 0) -> dict:
    key_of = jax.random.split(jax.random.key(seed), 8)
    activations = noise(key_of[0], (SECTIONS, 2, TOKENS, D), 1.0, 6.0, ((0, 4), (2, 4), (3, 2)))
    out_grad = noise(key_of[1], (SECTIONS, TOKENS, D), 0.25, 1.5, ((0, 4), (1, 4), (2, 2)))
    key_grad = noise(key_of[2], (SECTIONS, 2, TOKENS, KV_COLS), 0.25, 1.5, ((0, 4), (2, 4), (3, 2)))
    key_weight = noise(key_of[3], (SECTIONS, D, KV_COLS), KV_COLS ** -0.5, 0.25, ((0, 4), (1, 2)))
    plan = jax.vmap(lambda own: jax.random.permutation(own, 2))(jax.random.split(key_of[4], SECTIONS)).reshape((SECTIONS, 2)).astype(jnp.int32)
    first_moment = noise(key_of[5], (SECTIONS, GROUPS, FEAT, KV_COLS), 8.0, 48.0, ((0, 4), (1, 2), (2, 4)))
    second_moment = jnp.clip(jnp.exp(math.log(300.0) - 3.4011974 * jax.random.uniform(key_of[6], (SECTIONS, GROUPS, FEAT, KV_COLS), jnp.float32) ** block_scale(key_of[6], (SECTIONS, GROUPS, FEAT, KV_COLS), ((0, 4), (1, 2), (2, 4)), -0.2, 0.2)), 10.0, 300.0).astype(jnp.bfloat16)
    return {"activations": activations, "out_grad": out_grad, "key_grad": key_grad, "key_weight": key_weight, "plan": plan, "first_moment": first_moment, "second_moment": second_moment}


beta_one = 0.9
beta_two = 0.95
learn_rate = 0.01
weight_decay = 0.1
epsilon = 1e-08
first_fix = 1.0 - (0.9 ** 10) ** 10
second_fix = 1.0 - (0.95 ** 10) ** 10

def segment_grad(operands):
    incoming, key_rows, weight = operands
    added = jnp.dot(key_rows, weight.T, preferred_element_type=jnp.float32)
    return (incoming.astype(jnp.float32) + added).astype(jnp.bfloat16)

def update_section(operands):
    acts_here, keys_here, weight, first_old, second_old = operands
    gradient = jnp.einsum('mtf,mtc->fc', acts_here.astype(jnp.float32), keys_here.astype(jnp.float32), precision=lax.Precision.HIGHEST)
    gradient = gradient.reshape(GROUPS, FEAT, KV_COLS)
    old_weight = weight.astype(jnp.float32).reshape(GROUPS, FEAT, KV_COLS)
    first_fresh = beta_one * first_old.astype(jnp.float32) + (1.0 - beta_one) * gradient
    second_fresh = beta_two * second_old.astype(jnp.float32) + (1.0 - beta_two) * gradient * gradient
    update = first_fresh / first_fix / (jnp.sqrt(second_fresh / second_fix) + epsilon) + weight_decay * old_weight
    new_weight = (old_weight - learn_rate * update).astype(jnp.bfloat16)
    checksum = lax.optimization_barrier(jnp.mean(gradient.reshape(GROUPS, N_DP, FEAT // N_DP, KV_COLS), axis=2))
    return (new_weight, first_fresh.astype(jnp.bfloat16), second_fresh.astype(jnp.bfloat16), checksum)

def reference(activations, out_grad, key_grad, key_weight, plan, first_moment, second_moment):
    early_index = plan[:, 0].astype(jnp.int32)[:, None, None, None]
    late_index = plan[:, 1].astype(jnp.int32)[:, None, None, None]
    early_keys = jnp.take_along_axis(key_grad, early_index, axis=1)[:, 0]
    late_keys = jnp.take_along_axis(key_grad, late_index, axis=1)[:, 0]
    first_pass = lax.map(segment_grad, (out_grad, early_keys, key_weight))
    received = jnp.roll(first_pass, -1, axis=0)
    second_pass = lax.map(segment_grad, (received, late_keys, key_weight))
    received_grad = jnp.roll(second_pass, -1, axis=0)
    new_weight, new_first, new_second, checksum = lax.map(update_section, (activations, key_grad, key_weight, first_moment, second_moment))
    return (received_grad, new_weight, new_first, new_second, checksum)
```

```python
import functools

import jax
import jax.numpy as jnp
from jax import lax
from jax.experimental import pallas as pl
from jax.experimental.pallas import tpu as pltpu
from jax.sharding import PartitionSpec as P

beta_one = 0.9
beta_two = 0.95
learn_rate = 0.01
weight_decay = 0.1
epsilon = 1e-08
first_fix = 1.0 - (0.9**10) ** 10
second_fix = 1.0 - (0.95**10) ** 10


INWARD = [(0, 1), (3, 2)]
ACROSS = [(1, 2), (2, 1)]
OUTWARD = [(1, 0), (2, 3)]
PIECES = 2


def send_back(outgoing):
    count = lax.axis_size("pipe")
    pairs = [(source, (source - 1) % count) for source in range(count)]
    return lax.ppermute(outgoing, "pipe", pairs)


def all_heads(keys):
    count = lax.axis_size("head")
    if count != 2:
        return lax.all_gather(keys, "head", axis=2, tiled=True)
    other = lax.ppermute(keys, "head", [(0, 1), (1, 0)])
    first = lax.axis_index("head") == 0
    return jnp.concatenate(
        [jnp.where(first, keys, other), jnp.where(first, other, keys)], axis=2
    )


def outer(rows_ref, keys_ref):
    micro, tokens, rows = rows_ref.shape
    columns = keys_ref.shape[2]
    return lax.dot_general(
        rows_ref[...].reshape(micro * tokens, rows),
        keys_ref[...].reshape(micro * tokens, columns),
        (((0,), (0,)), ((), ())),
        preferred_element_type=jnp.float32,
    )


def pair_kernel(at_ref, acts_ref, keys_ref, far_acts_ref, far_keys_ref, out_ref):
    total = outer(acts_ref, keys_ref) + outer(far_acts_ref, far_keys_ref)
    out_ref[...] = total.astype(out_ref.dtype)


def add_kernel(at_ref, acts_ref, keys_ref, sum_ref, out_ref):
    total = outer(acts_ref, keys_ref) + sum_ref[...].astype(jnp.float32)
    out_ref[...] = total.astype(out_ref.dtype)


def update_kernel(
    scale,
    carried,
    at_ref,
    acts_ref,
    keys_ref,
    far_acts_ref,
    far_keys_ref,
    across_ref,
    outward_ref,
    weight_ref,
    first_ref,
    second_ref,
    *refs,
):
    new_weight_ref, new_first_ref, new_second_ref, column_ref = refs[-4:]
    gradient = (
        outer(acts_ref, keys_ref)
        + outer(far_acts_ref, far_keys_ref)
        + across_ref[...].astype(jnp.float32)
        + outward_ref[...].astype(jnp.float32)
    )
    columns = jnp.sum(gradient, axis=0, keepdims=True)
    if carried:
        columns = columns + refs[0][...]
    column_ref[...] = columns * scale
    old_weight = weight_ref[...].astype(jnp.float32)
    first_fresh = beta_one * first_ref[...].astype(jnp.float32) + (1.0 - beta_one) * gradient
    second_fresh = (
        beta_two * second_ref[...].astype(jnp.float32) + (1.0 - beta_two) * gradient * gradient
    )
    update = (
        first_fresh
        * (1.0 / first_fix)
        / (jnp.sqrt(second_fresh * (1.0 / second_fix)) + epsilon)
        + weight_decay * old_weight
    )
    new_weight_ref[...] = (old_weight - learn_rate * update).astype(new_weight_ref.dtype)
    new_first_ref[...] = first_fresh.astype(new_first_ref.dtype)
    new_second_ref[...] = second_fresh.astype(new_second_ref.dtype)


def body(activations, out_grad, key_grad, key_weight, plan, first_moment, second_moment):
    assert lax.axis_size("dp") == 4
    acts = activations[0]
    weight = key_weight[0]
    micro, tokens, feats = acts.shape
    columns = weight.shape[1]
    shard_rows = first_moment.shape[2]
    piece = shard_rows // PIECES
    place = lax.axis_index("dp")
    mirrored = place >= 2
    is_end = (place == 0) | (place == 3)

    def block_of(shard, part):
        return jnp.where(mirrored, 3 - shard, shard) * PIECES + part

    near_keys = key_grad[0]
    far_near_keys = lax.ppermute(near_keys, "dp", INWARD)
    all_keys = all_heads(near_keys)
    far_acts = {}
    for shard in (3, 2, 1):
        for part in range(PIECES):
            rows = lax.dynamic_slice_in_dim(acts, block_of(shard, part) * piece, piece, 2)
            far_acts[shard, part] = lax.ppermute(rows, "dp", INWARD)
    far_keys = all_heads(far_near_keys)

    early_keys = lax.dynamic_index_in_dim(all_keys, plan[0, 0], 0, keepdims=False)
    late_keys = lax.dynamic_index_in_dim(all_keys, plan[0, 1], 0, keepdims=False)

    def through(incoming, key_rows):
        added = lax.dot_general(
            key_rows, weight, (((1,), (1,)), ((), ())), preferred_element_type=jnp.float32
        )
        return (incoming.astype(jnp.float32) + added).astype(jnp.bfloat16)

    received = send_back(through(out_grad[0], early_keys))
    passed = send_back(through(received, late_keys))

    acts_spec = pl.BlockSpec((micro, tokens, piece), lambda g, at: (0, 0, at[0]))
    keys_spec = pl.BlockSpec((micro, tokens, columns), lambda g, at: (0, 0, 0))
    far_spec = pl.BlockSpec((micro, tokens, piece), lambda g, at: (0, 0, 0))
    sum_spec = pl.BlockSpec((piece, columns), lambda g, at: (0, 0))
    params = pltpu.CompilerParams(vmem_limit_bytes=32 * 1024 * 1024)

    def cost(products, arrays):
        return pl.CostEstimate(
            flops=2 * products * micro * tokens * piece * columns,
            bytes_accessed=2 * arrays * piece * columns,
            transcendentals=0,
        )

    def pair_sum(shard, part):
        return pl.pallas_call(
            pair_kernel,
            grid_spec=pltpu.PrefetchScalarGridSpec(
                num_scalar_prefetch=1,
                grid=(1,),
                in_specs=[acts_spec, keys_spec, far_spec, keys_spec],
                out_specs=sum_spec,
            ),
            out_shape=jax.ShapeDtypeStruct((piece, columns), jnp.bfloat16),
            compiler_params=params,
            cost_estimate=cost(2, 5),
            name="pair_sum",
        )(block_of(shard, part)[None], acts, all_keys, far_acts[shard, part], far_keys)

    def add_own(part, arrived):
        return pl.pallas_call(
            add_kernel,
            grid_spec=pltpu.PrefetchScalarGridSpec(
                num_scalar_prefetch=1,
                grid=(1,),
                in_specs=[acts_spec, keys_spec, sum_spec],
                out_specs=sum_spec,
            ),
            out_shape=jax.ShapeDtypeStruct((piece, columns), jnp.bfloat16),
            compiler_params=params,
            cost_estimate=cost(1, 4),
            name="add_own",
        )(block_of(0, part)[None], acts, all_keys, arrived)

    across = {}
    for shard in (3, 2):
        for part in range(PIECES):
            across[3 - shard, part] = lax.ppermute(pair_sum(shard, part), "dp", ACROSS)
    outward = {}
    for part in range(PIECES):
        outward[part] = lax.ppermute(add_own(part, across[0, part]), "dp", OUTWARD)

    shape = jax.ShapeDtypeStruct((shard_rows, columns), jnp.bfloat16)
    results = None
    for part in range(PIECES):
        carried = results is not None
        half_spec = pl.BlockSpec((piece, columns), lambda g, at, part=part: (part, 0))
        column_spec = pl.BlockSpec((1, columns), lambda g, at: (0, 0))
        in_specs = [
            acts_spec,
            keys_spec,
            far_spec,
            keys_spec,
            sum_spec,
            sum_spec,
            pl.BlockSpec((piece, columns), lambda g, at: (at[0], 0)),
            half_spec,
            half_spec,
        ]
        operands = [
            acts,
            all_keys,
            far_acts[1, part],
            far_keys,
            across[1, part],
            outward[part],
            weight,
            first_moment[0, 0],
            second_moment[0, 0],
        ]
        aliases = {}
        if carried:
            in_specs += [column_spec] + [pl.BlockSpec(memory_space=pl.ANY)] * 3
            operands += [results[3], *results[:3]]
            aliases = {11: 0, 12: 1, 13: 2}
        last = part == PIECES - 1
        own = place * PIECES + part
        results = pl.pallas_call(
            functools.partial(update_kernel, 1.0 / shard_rows if last else 1.0, carried),
            grid_spec=pltpu.PrefetchScalarGridSpec(
                num_scalar_prefetch=1,
                grid=(1,),
                in_specs=in_specs,
                out_specs=[half_spec, half_spec, half_spec, column_spec],
            ),
            out_shape=[shape, shape, shape, jax.ShapeDtypeStruct((1, columns), jnp.float32)],
            input_output_aliases=aliases,
            compiler_params=params,
            cost_estimate=cost(2, 10),
            name="update",
        )(own[None], *operands)
    new_weight, new_first, new_second, checksum = results
    return (
        passed[None],
        new_weight[None, None],
        new_first[None, None],
        new_second[None, None],
        checksum[None, None],
    )


def solution(mesh):
    return jax.shard_map(
        body,
        mesh=mesh,
        in_specs=(
            P("pipe", None, "dp", "head"),
            P("pipe", "dp", "head"),
            P("pipe", None, "dp", "head"),
            P("pipe", "head", None),
            P("pipe", None),
            P("pipe", "head", "dp", None),
            P("pipe", "head", "dp", None),
        ),
        out_specs=(
            P("pipe", "dp", "head"),
            P("pipe", "head", "dp", None),
            P("pipe", "head", "dp", None),
            P("pipe", "head", "dp", None),
            P("pipe", "head", "dp", None),
        ),
        check_vma=False,
    )
```

```python
import functools

import jax
import jax.numpy as jnp
from jax import lax
from jax.experimental import pallas as pl
from jax.experimental.pallas import tpu as pltpu
from jax.sharding import PartitionSpec as P


beta_one = 0.9
beta_two = 0.95
learn_rate = 0.01
weight_decay = 0.1
epsilon = 1e-08
first_fix = 1.0 - (0.9**10) ** 10
second_fix = 1.0 - (0.95**10) ** 10


INWARD = [(0, 1), (3, 2)]
ACROSS = [(1, 2), (2, 1)]
OUTWARD = [(1, 0), (2, 3)]
PARAMS = pltpu.CompilerParams(vmem_limit_bytes=24 * 1024 * 1024)
CUT_PARAMS = pltpu.CompilerParams(vmem_limit_bytes=64_000_000)
LOAD_PARAMS = pltpu.CompilerParams(vmem_limit_bytes=52_000_000)
IN_VMEM = pl.BlockSpec(memory_space=pltpu.VMEM)
ANYWHERE = pl.BlockSpec(memory_space=pl.ANY)


def shard_at(place, shard):
    return jnp.where(place >= 2, 3 - shard, shard)


def outer(rows_ref, keys_ref):
    micro, tokens, rows = rows_ref.shape
    columns = keys_ref.shape[2]
    return lax.dot_general(
        rows_ref[...].reshape(micro * tokens, rows),
        keys_ref[...].reshape(micro * tokens, columns),
        (((0,), (0,)), ((), ())),
        preferred_element_type=jnp.float32,
    )


def pair_kernel(at_ref, acts_ref, keys_ref, far_acts_ref, far_keys_ref, out_ref):
    total = outer(acts_ref, keys_ref) + outer(far_acts_ref, far_keys_ref)
    out_ref[...] = total.astype(out_ref.dtype)


def add_kernel(at_ref, acts_ref, keys_ref, *refs):
    sum_refs, out_ref = refs[:-1], refs[-1]
    total = outer(acts_ref, keys_ref)
    start = 0
    for sum_ref in sum_refs:
        rows = sum_ref.shape[0]
        part = total[start : start + rows] + sum_ref[...].astype(jnp.float32)
        out_ref[start : start + rows, :] = part.astype(out_ref.dtype)
        start += rows


def update_kernel(
    scale,
    carried,
    at_ref,
    acts_ref,
    keys_ref,
    far_acts_ref,
    far_keys_ref,
    across_ref,
    outward_ref,
    weight_ref,
    first_ref,
    second_ref,
    *refs,
):
    new_weight_ref, new_first_ref, new_second_ref, column_ref = refs[-4:]
    gradient = (
        outer(acts_ref, keys_ref)
        + outer(far_acts_ref, far_keys_ref)
        + across_ref[...].astype(jnp.float32)
        + outward_ref[...].astype(jnp.float32)
    )
    columns = jnp.sum(gradient, axis=0, keepdims=True)
    if carried:
        columns = columns + refs[0][...]
    column_ref[...] = columns * scale
    old_weight = weight_ref[...].astype(jnp.float32)
    first_fresh = beta_one * first_ref[...].astype(jnp.float32) + (1.0 - beta_one) * gradient
    second_fresh = (
        beta_two * second_ref[...].astype(jnp.float32) + (1.0 - beta_two) * gradient * gradient
    )
    fixed = second_fresh * (1.0 / second_fix)
    step = first_fresh * (learn_rate / first_fix) / (fixed * lax.rsqrt(fixed) + epsilon)
    new_weight = old_weight * (1.0 - learn_rate * weight_decay) - step
    new_weight_ref[...] = new_weight.astype(new_weight_ref.dtype)
    new_first_ref[...] = first_fresh.astype(new_first_ref.dtype)
    new_second_ref[...] = second_fresh.astype(new_second_ref.dtype)


def slice_kernel(rows_in_shard, wanted, at_ref, acts_ref, *refs):
    outs, sem = refs[: len(wanted)], refs[len(wanted)]
    copies = []
    for index, (shard, offset, size) in enumerate(wanted):
        start = pl.multiple_of(shard_at(at_ref[0], shard) * rows_in_shard + offset, size)
        copies.append(
            pltpu.make_async_copy(
                acts_ref.at[:, :, pl.ds(start, size)], outs[index], sem.at[index]
            )
        )
    for copy in copies:
        copy.start()
    for copy in copies:
        copy.wait()


def relay_kernel(parts, plan_ref, keys_ref, incoming_ref, weight_ref, out_ref):
    width = weight_ref.shape[0] // parts
    for index in range(parts):
        part = pl.ds(index * width, width)
        added = lax.dot_general(
            keys_ref[0],
            weight_ref[part, :],
            (((1,), (1,)), ((), ())),
            preferred_element_type=jnp.float32,
        )
        total = incoming_ref[:, part].astype(jnp.float32) + added
        out_ref[:, part] = total.astype(out_ref.dtype)


def load_kernel(at_ref, source_ref, target_ref, sem):
    copy = pltpu.make_async_copy(source_ref, target_ref, sem)
    copy.start()
    copy.wait()


def copy_kernel(pieces, source_ref, target_ref, buffer, in_sem, out_sem):
    rows = source_ref.shape[0] // pieces
    ins, outs = [], []
    for index in range(pieces):
        part = pl.ds(index * rows, rows)
        ins.append(
            pltpu.make_async_copy(source_ref.at[part], buffer.at[part], in_sem.at[index])
        )
        outs.append(
            pltpu.make_async_copy(buffer.at[part], target_ref.at[part], out_sem.at[index])
        )
    for copy in ins:
        copy.start()
    for arriving, leaving in zip(ins, outs):
        arriving.wait()
        leaving.start()
    for copy in outs:
        copy.wait()


def copied(array):
    pieces = 7 if array.shape[0] % (7 * 16) == 0 else 1
    return pl.pallas_call(
        functools.partial(copy_kernel, pieces),
        in_specs=[ANYWHERE],
        out_specs=ANYWHERE,
        out_shape=jax.ShapeDtypeStruct(array.shape, array.dtype),
        scratch_shapes=[
            pltpu.VMEM(array.shape, array.dtype),
            pltpu.SemaphoreType.DMA((pieces,)),
            pltpu.SemaphoreType.DMA((pieces,)),
        ],
        compiler_params=PARAMS,
        cost_estimate=pl.CostEstimate(
            flops=0, bytes_accessed=4 * array.size, transcendentals=0
        ),
        name="copied",
    )(array)


def body(activations, out_grad, key_grad, key_weight, plan, first_moment, second_moment):
    assert lax.axis_size("dp") == 4
    acts = activations[0]
    weight = key_weight[0]
    micro, tokens, feats = acts.shape
    columns = weight.shape[1]
    shard_rows = first_moment.shape[2]
    half, quarter = shard_rows // 2, shard_rows // 4
    halves = [(0, half), (half, half)]
    coarse, fine, finest = halves, halves, halves
    if quarter % 256 == 0:
        coarse = [(0, quarter), (quarter, quarter), (half, half)]
        fine = [(0, half), (half, quarter), (half + quarter, quarter)]
        eighth = quarter // 2
        finest = fine[:2] + [(half + quarter, eighth), (half + quarter + eighth, eighth)]
    far_pieces = {3: coarse, 2: halves, 1: finest}
    across_pieces = {0: coarse, 1: fine}
    where_am_i = lax.axis_index("dp")[None]

    def all_heads(keys, before=None):
        count = lax.axis_size("head")
        if count != 2:
            return lax.all_gather(keys, "head", axis=2, tiled=True)
        other = lax.ppermute(keys, "head", [(0, 1), (1, 0)])
        if before is not None:
            other, keys, _ = lax.optimization_barrier((other, keys, before))
        first = lax.axis_index("head") == 0
        return jnp.concatenate(
            [jnp.where(first, keys, other), jnp.where(first, other, keys)], axis=2
        )

    def call(kernel, specs, out_spec, shape, flops, operands, scalar=where_am_i, **more):
        moved = sum(array.size for array in jax.tree.leaves(shape)) * 6
        return pl.pallas_call(
            kernel,
            grid_spec=pltpu.PrefetchScalarGridSpec(
                num_scalar_prefetch=1,
                grid=more.pop("grid", (1,)),
                in_specs=specs,
                out_specs=out_spec,
                scratch_shapes=more.pop("scratch_shapes", ()),
            ),
            out_shape=shape,
            compiler_params=more.pop("params", PARAMS),
            cost_estimate=pl.CostEstimate(
                flops=flops, bytes_accessed=moved, transcendentals=0
            ),
            **more,
        )(scalar, *operands)

    def slices(wanted, params):
        parts = call(
            functools.partial(slice_kernel, shard_rows, wanted),
            [ANYWHERE],
            [IN_VMEM] * len(wanted),
            [
                jax.ShapeDtypeStruct((micro, tokens, size), acts.dtype)
                for _, _, size in wanted
            ],
            0,
            (acts,),
            scratch_shapes=[pltpu.SemaphoreType.DMA((len(wanted),))],
            params=params,
        )
        return {(shard, offset): part for (shard, offset, _), part in zip(wanted, parts)}

    near_keys = key_grad[0]
    far_near_keys = lax.ppermute(near_keys, "dp", INWARD)
    all_keys = all_heads(near_keys)
    wanted = [(shard, *piece) for shard in (3, 2, 1) for piece in far_pieces[shard]]
    outgoing = slices(wanted[:2], CUT_PARAMS) | slices(wanted[2:], PARAMS)
    far_acts = {}
    for shard in (3, 2, 1):
        for offset, size in far_pieces[shard]:
            far_acts[shard, offset] = lax.ppermute(outgoing[shard, offset], "dp", INWARD)
    relay_shape = jax.ShapeDtypeStruct((tokens, feats), jnp.bfloat16)
    relay_flops = 2 * tokens * feats * columns

    def turn_keys(turn):
        return pl.BlockSpec((1, tokens, columns), lambda g, p: (p[turn], 0, 0))

    held_weight = call(
        load_kernel,
        [ANYWHERE],
        IN_VMEM,
        jax.ShapeDtypeStruct(weight.shape, weight.dtype),
        0,
        (weight,),
        scratch_shapes=[pltpu.SemaphoreType.DMA],
        params=LOAD_PARAMS,
    )

    def through(incoming, turn):
        return call(
            functools.partial(relay_kernel, 2),
            [turn_keys(turn), IN_VMEM, IN_VMEM],
            IN_VMEM,
            relay_shape,
            relay_flops,
            (all_keys, incoming, held_weight),
            scalar=plan[0],
        )

    count = lax.axis_size("pipe")
    back = [(source, (source - 1) % count) for source in range(count)]
    passing = through(out_grad[0], 0)
    received = lax.ppermute(passing, "pipe", back)
    passed = copied(lax.ppermute(through(received, 1), "pipe", back))
    far_keys = all_heads(far_near_keys, passing)

    keys_spec = pl.BlockSpec((micro, tokens, columns), lambda g, at: (0, 0, 0))

    def acts_spec(shard, offset, size):
        per_shard = shard_rows // size
        return pl.BlockSpec(
            (micro, tokens, size),
            lambda g, at: (0, 0, shard_at(at[0], shard) * per_shard + offset // size),
        )

    def holder(pieces, offset):
        return max(start for start, _ in pieces if start <= offset)

    def far_spec(shard, offset, size):
        block = (offset - holder(far_pieces[shard], offset)) // size
        return pl.BlockSpec((micro, tokens, size), lambda g, at: (0, 0, block))

    def far_piece(shard, offset):
        return far_acts[shard, holder(far_pieces[shard], offset)]

    def sum_spec(size, block=0):
        return pl.BlockSpec((size, columns), lambda g, at: (block, 0))

    def product(size, terms):
        return 2 * terms * micro * tokens * size * columns

    def pair_sum(shard, offset, size):
        return call(
            pair_kernel,
            [
                acts_spec(shard, offset, size),
                keys_spec,
                far_spec(shard, offset, size),
                keys_spec,
            ],
            sum_spec(size),
            jax.ShapeDtypeStruct((size, columns), jnp.bfloat16),
            product(size, 2),
            (acts, all_keys, far_piece(shard, offset), far_keys),
        )

    def add_own(offset, size, arrived):
        return call(
            add_kernel,
            [acts_spec(0, offset, size), keys_spec] + [sum_spec(part.shape[0]) for part in arrived],
            sum_spec(size),
            jax.ShapeDtypeStruct((size, columns), jnp.bfloat16),
            product(size, 1),
            (acts, all_keys, *arrived),
        )

    across = {}
    for shard in (0, 1):
        for offset, size in across_pieces[shard]:
            total = pair_sum(3 - shard, offset, size)
            across[shard, offset] = lax.ppermute(total, "dp", ACROSS)
    outward = {}
    for offset, size in halves:
        arrived = [
            across[0, start] for start, _ in coarse if offset <= start < offset + size
        ]
        outward[offset] = lax.ppermute(add_own(offset, size, arrived), "dp", OUTWARD)

    shape = jax.ShapeDtypeStruct((shard_rows, columns), jnp.bfloat16)
    column_spec = pl.BlockSpec((1, columns), lambda g, at: (0, 0))
    results, copied_yet = None, False
    for offset, size in finest:
        last = offset + size == shard_rows
        here = where_am_i
        if results is not None and not copied_yet:
            copied_yet = True
            here, passed = lax.optimization_barrier((where_am_i, passed))
        block, per_shard = offset // size, shard_rows // size
        held, near = holder(halves, offset), holder(across_pieces[1], offset)

        def own_rows(g, at, block=block, per_shard=per_shard):
            return at[0] * per_shard + block

        specs = [
            pl.BlockSpec(
                (micro, tokens, size), lambda g, at, own=own_rows: (0, 0, own(g, at))
            ),
            keys_spec,
            far_spec(1, offset, size),
            keys_spec,
            sum_spec(size, (offset - near) // size),
            sum_spec(size, (offset - held) // size),
            pl.BlockSpec((size, columns), lambda g, at, own=own_rows: (own(g, at), 0)),
            sum_spec(size, block),
            sum_spec(size, block),
        ]
        operands = [
            acts,
            all_keys,
            far_piece(1, offset),
            far_keys,
            across[1, near],
            outward[held],
            weight,
            first_moment[0, 0],
            second_moment[0, 0],
        ]
        aliases = {}
        if results is not None:
            specs += [column_spec] + [ANYWHERE] * 3
            operands += [results[3], *results[:3]]
            aliases = {11: 0, 12: 1, 13: 2}
        results = call(
            functools.partial(
                update_kernel, 1.0 / shard_rows if last else 1.0, results is not None
            ),
            specs,
            [sum_spec(size, block)] * 3 + [column_spec],
            [shape] * 3 + [jax.ShapeDtypeStruct((1, columns), jnp.float32)],
            product(size, 2),
            operands,
            scalar=here,
            input_output_aliases=aliases,
        )
    new_weight, new_first, new_second, checksum = results
    return (
        passed[None],
        new_weight[None, None],
        new_first[None, None],
        new_second[None, None],
        checksum[None, None],
    )


def solution(mesh):
    return jax.shard_map(
        body,
        mesh=mesh,
        in_specs=(
            P("pipe", None, "dp", "head"),
            P("pipe", "dp", "head"),
            P("pipe", None, "dp", "head"),
            P("pipe", "head", None),
            P("pipe", None),
            P("pipe", "head", "dp", None),
            P("pipe", "head", "dp", None),
        ),
        out_specs=(
            P("pipe", "dp", "head"),
            P("pipe", "head", "dp", None),
            P("pipe", "head", "dp", None),
            P("pipe", "head", "dp", None),
            P("pipe", "head", "dp", None),
        ),
        check_vma=False,
    )
```

```python
import functools

import jax
import jax.numpy as jnp
from jax import lax
from jax.experimental import pallas as pl
from jax.experimental.pallas import tpu as pltpu
from jax.sharding import PartitionSpec as P


beta_one = 0.9
beta_two = 0.95
learn_rate = 0.01
weight_decay = 0.1
epsilon = 1e-08
first_fix = 1.0 - (0.9**10) ** 10
second_fix = 1.0 - (0.95**10) ** 10


INWARD = [(0, 1), (3, 2)]
ACROSS = [(1, 2), (2, 1)]
OUTWARD = [(1, 0), (2, 3)]
PARAMS = pltpu.CompilerParams(vmem_limit_bytes=24 * 1024 * 1024)
CUT_PARAMS = pltpu.CompilerParams(vmem_limit_bytes=64_000_000)
LOAD_PARAMS = pltpu.CompilerParams(vmem_limit_bytes=52_000_000)
CHUNK = 128
IN_VMEM = pl.BlockSpec(memory_space=pltpu.VMEM)
ANYWHERE = pl.BlockSpec(memory_space=pl.ANY)


def shard_at(place, shard):
    return jnp.where(place >= 2, 3 - shard, shard)


def outer(rows_ref, keys_ref):
    micro, tokens, rows = rows_ref.shape
    columns = keys_ref.shape[2]
    return lax.dot_general(
        rows_ref[...].reshape(micro * tokens, rows),
        keys_ref[...].reshape(micro * tokens, columns),
        (((0,), (0,)), ((), ())),
        preferred_element_type=jnp.float32,
    )


def own_rows(acts_ref, start, size):
    return acts_ref.at[:, :, pl.ds(pl.multiple_of(start, 128), size)]


def pair_kernel(start_of, far_start, at_ref, acts_ref, keys_ref, far_acts_ref, far_keys_ref, out_ref):
    size = out_ref.shape[0]
    acts = own_rows(acts_ref, start_of(at_ref[0]), size)
    far_acts = far_acts_ref.at[:, :, pl.ds(far_start, size)]
    total = outer(acts, keys_ref) + outer(far_acts, far_keys_ref)
    out_ref[...] = total.astype(out_ref.dtype)


def add_kernel(start_of, at_ref, acts_ref, keys_ref, *refs):
    sum_refs, out_ref = refs[:-1], refs[-1]
    total = outer(own_rows(acts_ref, start_of(at_ref[0]), out_ref.shape[0]), keys_ref)
    start = 0
    for sum_ref in sum_refs:
        rows = sum_ref.shape[0]
        part = total[start : start + rows] + sum_ref[...].astype(jnp.float32)
        out_ref[start : start + rows, :] = part.astype(out_ref.dtype)
        start += rows


def update_kernel(
    offset,
    outward_starts,
    carried,
    last,
    at_ref,
    acts_ref,
    keys_ref,
    far_acts_ref,
    far_keys_ref,
    across_ref,
    weight_ref,
    first_ref,
    second_ref,
    *refs,
):
    outward_refs = refs[: len(outward_starts)]
    *out_refs, column_ref, total_ref, staged_ref, sum_ref, sem, sum_sem = refs[-9:]
    size, shard_rows = across_ref.shape[0], first_ref.shape[0]
    scale = 1.0 / shard_rows if last else 1.0
    own = at_ref[0] * shard_rows + offset
    total_ref[...] = outer(own_rows(acts_ref, own, size), keys_ref) + outer(
        far_acts_ref, far_keys_ref
    )
    columns = refs[len(outward_starts)][...] if carried else 0.0
    copies = []
    for index, row in enumerate(range(0, size, CHUNK)):
        here = pl.ds(row, CHUNK)
        there = pl.ds(offset + row, CHUNK)
        piece = max(
            number for number, start in enumerate(outward_starts) if start <= offset + row
        )
        arrived = pl.ds(offset + row - outward_starts[piece], CHUNK)
        gradient = (
            total_ref[here, :]
            + across_ref[here, :].astype(jnp.float32)
            + outward_refs[piece][arrived, :].astype(jnp.float32)
        )
        columns = columns + jnp.sum(gradient, axis=0, keepdims=True)
        old_weight = weight_ref[pl.ds(pl.multiple_of(own + row, CHUNK), CHUNK), :].astype(
            jnp.float32
        )
        first_fresh = (
            beta_one * first_ref[there, :].astype(jnp.float32) + (1.0 - beta_one) * gradient
        )
        second_fresh = (
            beta_two * second_ref[there, :].astype(jnp.float32)
            + (1.0 - beta_two) * gradient * gradient
        )
        fixed = second_fresh * (1.0 / second_fix)
        step = first_fresh * (learn_rate / first_fix) / (fixed * lax.rsqrt(fixed) + epsilon)
        new_weight = old_weight * (1.0 - learn_rate * weight_decay) - step
        for which, value in enumerate((new_weight, first_fresh, second_fresh)):
            staged_ref[which, here, :] = value.astype(staged_ref.dtype)
            copy = pltpu.make_async_copy(
                staged_ref.at[which, here], out_refs[which].at[there], sem.at[which, index]
            )
            copy.start()
            copies.append(copy)
    sum_ref[...] = columns * scale
    if last:
        copies.append(pltpu.make_async_copy(sum_ref, column_ref, sum_sem))
        copies[-1].start()
    else:
        column_ref[...] = sum_ref[...]
    for copy in copies:
        copy.wait()


def slice_kernel(rows_in_shard, wanted, at_ref, acts_ref, *refs):
    outs, sem = refs[: len(wanted)], refs[len(wanted)]
    copies = []
    for index, (shard, offset, size) in enumerate(wanted):
        start = pl.multiple_of(shard_at(at_ref[0], shard) * rows_in_shard + offset, 128)
        copies.append(
            pltpu.make_async_copy(
                acts_ref.at[:, :, pl.ds(start, size)], outs[index], sem.at[index]
            )
        )
    for copy in copies:
        copy.start()
    for copy in copies:
        copy.wait()


def relay_kernel(parts, plan_ref, keys_ref, incoming_ref, weight_ref, out_ref):
    width = weight_ref.shape[0] // parts
    for index in range(parts):
        part = pl.ds(index * width, width)
        added = lax.dot_general(
            keys_ref[0],
            weight_ref[part, :],
            (((1,), (1,)), ((), ())),
            preferred_element_type=jnp.float32,
        )
        total = incoming_ref[:, part].astype(jnp.float32) + added
        out_ref[:, part] = total.astype(out_ref.dtype)


def load_kernel(at_ref, source_ref, target_ref, sem):
    copy = pltpu.make_async_copy(source_ref, target_ref, sem)
    copy.start()
    copy.wait()


def copy_kernel(pieces, source_ref, target_ref, buffer, in_sem, out_sem):
    rows = source_ref.shape[0] // pieces
    ins, outs = [], []
    for index in range(pieces):
        part = pl.ds(index * rows, rows)
        ins.append(
            pltpu.make_async_copy(source_ref.at[part], buffer.at[part], in_sem.at[index])
        )
        outs.append(
            pltpu.make_async_copy(buffer.at[part], target_ref.at[part], out_sem.at[index])
        )
    for copy in ins:
        copy.start()
    for arriving, leaving in zip(ins, outs):
        arriving.wait()
        leaving.start()
    for copy in outs:
        copy.wait()


def copied(array):
    pieces = 7 if array.shape[0] % (7 * 16) == 0 else 1
    return pl.pallas_call(
        functools.partial(copy_kernel, pieces),
        in_specs=[ANYWHERE],
        out_specs=ANYWHERE,
        out_shape=jax.ShapeDtypeStruct(array.shape, array.dtype),
        scratch_shapes=[
            pltpu.VMEM(array.shape, array.dtype),
            pltpu.SemaphoreType.DMA((pieces,)),
            pltpu.SemaphoreType.DMA((pieces,)),
        ],
        compiler_params=PARAMS,
        cost_estimate=pl.CostEstimate(
            flops=0, bytes_accessed=4 * array.size, transcendentals=0
        ),
        name="copied",
    )(array)


def body(activations, out_grad, key_grad, key_weight, plan, first_moment, second_moment):
    assert lax.axis_size("dp") == 4
    acts = activations[0]
    weight = key_weight[0]
    micro, tokens, feats = acts.shape
    columns = weight.shape[1]
    shard_rows = first_moment.shape[2]
    half = shard_rows // 2
    halves = [(0, half), (half, half)]
    head_pieces, tail_pieces, outward_pieces = halves, halves, halves
    if shard_rows % 1024 == 0:
        eighth = shard_rows // 8
        head_pieces = [(0, 2 * eighth), (2 * eighth, 3 * eighth), (5 * eighth, 3 * eighth)]
        tail_pieces = [(0, 4 * eighth), (4 * eighth, 3 * eighth), (7 * eighth, eighth)]
        outward_pieces = head_pieces
    far_pieces = {3: head_pieces, 2: halves, 1: tail_pieces}
    across_pieces = {0: head_pieces, 1: tail_pieces}
    where_am_i = lax.axis_index("dp")[None]

    def all_heads(keys, before=None):
        count = lax.axis_size("head")
        if count != 2:
            return lax.all_gather(keys, "head", axis=2, tiled=True)
        other = lax.ppermute(keys, "head", [(0, 1), (1, 0)])
        if before is not None:
            other, keys, _ = lax.optimization_barrier((other, keys, before))
        first = lax.axis_index("head") == 0
        return jnp.concatenate(
            [jnp.where(first, keys, other), jnp.where(first, other, keys)], axis=2
        )

    def call(kernel, specs, out_spec, shape, flops, operands, scalar=where_am_i, **more):
        moved = sum(array.size for array in jax.tree.leaves(shape)) * 6
        return pl.pallas_call(
            kernel,
            grid_spec=pltpu.PrefetchScalarGridSpec(
                num_scalar_prefetch=1,
                grid=more.pop("grid", (1,)),
                in_specs=specs,
                out_specs=out_spec,
                scratch_shapes=more.pop("scratch_shapes", ()),
            ),
            out_shape=shape,
            compiler_params=more.pop("params", PARAMS),
            cost_estimate=pl.CostEstimate(
                flops=flops, bytes_accessed=moved, transcendentals=0
            ),
            **more,
        )(scalar, *operands)

    def slices(wanted, params):
        parts = call(
            functools.partial(slice_kernel, shard_rows, wanted),
            [ANYWHERE],
            [IN_VMEM] * len(wanted),
            [
                jax.ShapeDtypeStruct((micro, tokens, size), acts.dtype)
                for _, _, size in wanted
            ],
            0,
            (acts,),
            scratch_shapes=[pltpu.SemaphoreType.DMA((len(wanted),))],
            params=params,
        )
        return {(shard, offset): part for (shard, offset, _), part in zip(wanted, parts)}

    near_keys = key_grad[0]
    far_near_keys = lax.ppermute(near_keys, "dp", INWARD)
    all_keys = all_heads(near_keys)
    wanted = [(shard, *piece) for shard in (3, 2, 1) for piece in far_pieces[shard]]
    outgoing = slices(wanted[:2], CUT_PARAMS) | slices(wanted[2:], PARAMS)
    far_acts = {}
    for shard in (3, 2, 1):
        for offset, size in far_pieces[shard]:
            far_acts[shard, offset] = lax.ppermute(outgoing[shard, offset], "dp", INWARD)
    relay_shape = jax.ShapeDtypeStruct((tokens, feats), jnp.bfloat16)
    relay_flops = 2 * tokens * feats * columns

    def turn_keys(turn):
        return pl.BlockSpec((1, tokens, columns), lambda g, p: (p[turn], 0, 0))

    held_weight = call(
        load_kernel,
        [ANYWHERE],
        IN_VMEM,
        jax.ShapeDtypeStruct(weight.shape, weight.dtype),
        0,
        (weight,),
        scratch_shapes=[pltpu.SemaphoreType.DMA],
        params=LOAD_PARAMS,
    )

    def through(incoming, turn):
        return call(
            functools.partial(relay_kernel, 2),
            [turn_keys(turn), IN_VMEM, IN_VMEM],
            IN_VMEM,
            relay_shape,
            relay_flops,
            (all_keys, incoming, held_weight),
            scalar=plan[0],
        )

    count = lax.axis_size("pipe")
    back = [(source, (source - 1) % count) for source in range(count)]
    passing = through(out_grad[0], 0)
    received = lax.ppermute(passing, "pipe", back)
    passed = copied(lax.ppermute(through(received, 1), "pipe", back))
    far_keys = all_heads(far_near_keys, passing)

    def holder(pieces, offset):
        return max(start for start, _ in pieces if start <= offset)

    def start_of(shard, offset):
        return lambda place: shard_at(place, shard) * shard_rows + offset

    def product(size, terms):
        return 2 * terms * micro * tokens * size * columns

    def pair_sum(shard, offset, size):
        held = holder(far_pieces[shard], offset)
        return call(
            functools.partial(pair_kernel, start_of(shard, offset), offset - held),
            [IN_VMEM] * 4,
            IN_VMEM,
            jax.ShapeDtypeStruct((size, columns), jnp.bfloat16),
            product(size, 2),
            (acts, all_keys, far_acts[shard, held], far_keys),
        )

    def add_own(offset, size, arrived):
        return call(
            functools.partial(add_kernel, start_of(0, offset)),
            [IN_VMEM] * (2 + len(arrived)),
            IN_VMEM,
            jax.ShapeDtypeStruct((size, columns), jnp.bfloat16),
            product(size, 1),
            (acts, all_keys, *arrived),
        )

    across = {}
    for shard in (0, 1):
        for offset, size in across_pieces[shard]:
            total = pair_sum(3 - shard, offset, size)
            across[shard, offset] = lax.ppermute(total, "dp", ACROSS)
    outward = {}
    for offset, size in outward_pieces:
        arrived = [
            across[0, start] for start, _ in head_pieces if offset <= start < offset + size
        ]
        outward[offset] = lax.ppermute(add_own(offset, size, arrived), "dp", OUTWARD)

    shape = jax.ShapeDtypeStruct((shard_rows, columns), jnp.bfloat16)
    results = None
    for index, (offset, size) in enumerate(tail_pieces):
        last = offset + size == shard_rows
        here = where_am_i
        if index == 1:
            here, passed = lax.optimization_barrier((where_am_i, passed))
        needed = [
            start
            for start, rows in outward_pieces
            if start < offset + size and offset < start + rows
        ]
        operands = [
            acts,
            all_keys,
            far_acts[1, offset],
            far_keys,
            across[1, offset],
            held_weight,
            first_moment[0, 0],
            second_moment[0, 0],
            *[outward[start] for start in needed],
        ]
        specs = [IN_VMEM] * len(operands)
        aliases = {}
        if results is not None:
            operands += [results[3], *results[:3]]
            specs += [IN_VMEM] + [ANYWHERE] * 3
            aliases = {len(operands) - 2 + which: which for which in range(3)}
        results = call(
            functools.partial(
                update_kernel,
                offset,
                needed,
                results is not None,
                last,
            ),
            specs,
            [ANYWHERE] * 3 + [ANYWHERE if last else IN_VMEM],
            [shape] * 3 + [jax.ShapeDtypeStruct((1, columns), jnp.float32)],
            product(size, 2),
            operands,
            scalar=here,
            input_output_aliases=aliases,
            scratch_shapes=[
                pltpu.VMEM((size, columns), jnp.float32),
                pltpu.VMEM((3, size, columns), jnp.bfloat16),
                pltpu.VMEM((1, columns), jnp.float32),
                pltpu.SemaphoreType.DMA((3, size // CHUNK)),
                pltpu.SemaphoreType.DMA,
            ],
        )
    new_weight, new_first, new_second, checksum = results
    return (
        passed[None],
        new_weight[None, None],
        new_first[None, None],
        new_second[None, None],
        checksum[None, None],
    )


def solution(mesh):
    return jax.shard_map(
        body,
        mesh=mesh,
        in_specs=(
            P("pipe", None, "dp", "head"),
            P("pipe", "dp", "head"),
            P("pipe", None, "dp", "head"),
            P("pipe", "head", None),
            P("pipe", None),
            P("pipe", "head", "dp", None),
            P("pipe", "head", "dp", None),
        ),
        out_specs=(
            P("pipe", "dp", "head"),
            P("pipe", "head", "dp", None),
            P("pipe", "head", "dp", None),
            P("pipe", "head", "dp", None),
            P("pipe", "head", "dp", None),
        ),
        check_vma=False,
    )
```

```python
import dataclasses
import functools

import jax
import jax.numpy as jnp
from jax import lax
from jax.experimental import pallas as pl
from jax.experimental.pallas import tpu as pltpu
from jax.sharding import PartitionSpec as P


beta_one = 0.9
beta_two = 0.95
learn_rate = 0.01
weight_decay = 0.1
epsilon = 1e-08
first_fix = 1.0 - (0.9**10) ** 10
second_fix = 1.0 - (0.95**10) ** 10


INWARD = [(0, 1), (3, 2)]
ACROSS = [(1, 2), (2, 1)]
OUTWARD = [(1, 0), (2, 3)]
PARAMS = pltpu.CompilerParams(vmem_limit_bytes=24 * 1024 * 1024)
CUT_PARAMS = pltpu.CompilerParams(vmem_limit_bytes=64_000_000)
LOAD_PARAMS = pltpu.CompilerParams(vmem_limit_bytes=52_000_000)
CHUNK = 128
IN_VMEM = pl.BlockSpec(memory_space=pltpu.VMEM)
ANYWHERE = pl.BlockSpec(memory_space=pl.ANY)


def shard_at(place, shard):
    return jnp.where(place >= 2, 3 - shard, shard)


def outer(rows_ref, keys_ref):
    micro, tokens, rows = rows_ref.shape
    columns = keys_ref.shape[2]
    return lax.dot_general(
        rows_ref[...].reshape(micro * tokens, rows),
        keys_ref[...].reshape(micro * tokens, columns),
        (((0,), (0,)), ((), ())),
        preferred_element_type=jnp.float32,
    )


def own_rows(acts_ref, start, size):
    return acts_ref.at[:, :, pl.ds(pl.multiple_of(start, 128), size)]


def pair_kernel(start_of, far_start, at_ref, acts_ref, keys_ref, far_acts_ref, far_keys_ref, out_ref):
    size = out_ref.shape[0]
    acts = own_rows(acts_ref, start_of(at_ref[0]), size)
    far_acts = far_acts_ref.at[:, :, pl.ds(far_start, size)]
    total = outer(acts, keys_ref) + outer(far_acts, far_keys_ref)
    out_ref[...] = total.astype(out_ref.dtype)


def add_kernel(start_of, at_ref, acts_ref, keys_ref, *refs):
    sum_refs, out_ref = refs[:-1], refs[-1]
    total = outer(own_rows(acts_ref, start_of(at_ref[0]), out_ref.shape[0]), keys_ref)
    start = 0
    for sum_ref in sum_refs:
        rows = sum_ref.shape[0]
        part = total[start : start + rows] + sum_ref[...].astype(jnp.float32)
        out_ref[start : start + rows, :] = part.astype(out_ref.dtype)
        start += rows


@dataclasses.dataclass(frozen=True)
class Update:
    at_end: bool
    offset: int
    size: int
    outward_starts: tuple = ()
    carried: bool = False
    stash: bool = False
    stashed: int = -1
    last: bool = False


def update_kernel(
    plan, at_ref, acts_ref, keys_ref, weight_ref, first_ref, second_ref, *refs
):
    taken = len(plan.outward_starts) if plan.at_end else 3
    terms, refs = refs[:taken], list(refs[taken:])
    carried_ref = refs.pop(0) if plan.carried else None
    stashed_refs = [refs.pop(0) for _ in range(3)] if plan.stashed >= 0 else []
    *out_refs, column_ref, total_ref, staged_ref, sum_ref, sem, old_sem, sum_sem = refs[-10:]
    shard_rows = first_ref.shape[0]
    offset, size = plan.offset, plan.size
    place = at_ref[0]
    own = place * shard_rows + offset
    is_end = (place == 0) | (place == 3)
    mine = is_end if plan.at_end else jnp.logical_not(is_end)

    def old_copies():
        return [
            pltpu.make_async_copy(
                ref,
                out_refs[which].at[pl.ds(plan.stashed, ref.shape[0])],
                old_sem.at[which],
            )
            for which, ref in enumerate(stashed_refs)
        ]

    def new_copies(row):
        return [
            pltpu.make_async_copy(
                staged_ref.at[which, pl.ds(row, CHUNK)],
                out_refs[which].at[pl.ds(offset + row, CHUNK)],
                sem.at[which, row // CHUNK],
            )
            for which in range(3)
        ]

    def finish():
        for copy in old_copies():
            copy.wait()
        if not plan.stash:
            for row in range(0, size, CHUNK):
                for copy in new_copies(row):
                    copy.wait()

    sum_ref[...] = carried_ref[...] if plan.carried else jnp.zeros_like(sum_ref)

    @pl.when(mine)
    def _():
        for copy in old_copies():
            copy.start()
        product = outer(own_rows(acts_ref, own, size), keys_ref)
        if not plan.at_end:
            product = product + outer(terms[0], terms[1])
        total_ref[...] = product
        for row in range(0, size, CHUNK):
            here = pl.ds(row, CHUNK)
            there = pl.ds(offset + row, CHUNK)
            if plan.at_end:
                starts = plan.outward_starts
                piece = max(n for n, start in enumerate(starts) if start <= offset + row)
                arrived = terms[piece][pl.ds(offset + row - starts[piece], CHUNK), :]
            else:
                arrived = terms[2][here, :]
            gradient = total_ref[here, :] + arrived.astype(jnp.float32)
            sum_ref[...] += jnp.sum(gradient, axis=0, keepdims=True)
            weight_rows = pl.ds(pl.multiple_of(own + row, CHUNK), CHUNK)
            old_weight = weight_ref[weight_rows, :].astype(jnp.float32)
            first_fresh = (
                beta_one * first_ref[there, :].astype(jnp.float32) + (1.0 - beta_one) * gradient
            )
            second_fresh = (
                beta_two * second_ref[there, :].astype(jnp.float32)
                + (1.0 - beta_two) * gradient * gradient
            )
            fixed = second_fresh * (1.0 / second_fix)
            step = first_fresh * (learn_rate / first_fix) / (fixed * lax.rsqrt(fixed) + epsilon)
            new_weight = old_weight * (1.0 - learn_rate * weight_decay) - step
            for which, value in enumerate((new_weight, first_fresh, second_fresh)):
                value = value.astype(staged_ref.dtype)
                if plan.stash:
                    out_refs[which][here, :] = value
                else:
                    staged_ref[which, here, :] = value
            if not plan.stash:
                for copy in new_copies(row):
                    copy.start()
        if not plan.last:
            finish()

    if plan.last:
        sum_ref[...] = sum_ref[...] * (1.0 / shard_rows)
        copy = pltpu.make_async_copy(sum_ref, column_ref, sum_sem)
        copy.start()
        pl.when(mine)(finish)
        copy.wait()
    else:
        column_ref[...] = sum_ref[...]


def slice_kernel(rows_in_shard, wanted, at_ref, acts_ref, *refs):
    outs, sem = refs[: len(wanted)], refs[len(wanted)]
    copies = []
    for index, (shard, offset, size) in enumerate(wanted):
        start = pl.multiple_of(shard_at(at_ref[0], shard) * rows_in_shard + offset, 128)
        copies.append(
            pltpu.make_async_copy(
                acts_ref.at[:, :, pl.ds(start, size)], outs[index], sem.at[index]
            )
        )
    for copy in copies:
        copy.start()
    for copy in copies:
        copy.wait()


def relay_kernel(parts, plan_ref, keys_ref, incoming_ref, weight_ref, out_ref):
    width = weight_ref.shape[0] // parts
    for index in range(parts):
        part = pl.ds(index * width, width)
        added = lax.dot_general(
            keys_ref[0],
            weight_ref[part, :],
            (((1,), (1,)), ((), ())),
            preferred_element_type=jnp.float32,
        )
        total = incoming_ref[:, part].astype(jnp.float32) + added
        out_ref[:, part] = total.astype(out_ref.dtype)


def load_kernel(at_ref, source_ref, target_ref, sem):
    copy = pltpu.make_async_copy(source_ref, target_ref, sem)
    copy.start()
    copy.wait()


def copy_kernel(pieces, source_ref, target_ref, buffer, in_sem, out_sem):
    rows = source_ref.shape[0] // pieces
    ins, outs = [], []
    for index in range(pieces):
        part = pl.ds(index * rows, rows)
        ins.append(
            pltpu.make_async_copy(source_ref.at[part], buffer.at[part], in_sem.at[index])
        )
        outs.append(
            pltpu.make_async_copy(buffer.at[part], target_ref.at[part], out_sem.at[index])
        )
    for copy in ins:
        copy.start()
    for arriving, leaving in zip(ins, outs):
        arriving.wait()
        leaving.start()
    for copy in outs:
        copy.wait()


def copied(array):
    pieces = 7 if array.shape[0] % (7 * 16) == 0 else 1
    return pl.pallas_call(
        functools.partial(copy_kernel, pieces),
        in_specs=[ANYWHERE],
        out_specs=ANYWHERE,
        out_shape=jax.ShapeDtypeStruct(array.shape, array.dtype),
        scratch_shapes=[
            pltpu.VMEM(array.shape, array.dtype),
            pltpu.SemaphoreType.DMA((pieces,)),
            pltpu.SemaphoreType.DMA((pieces,)),
        ],
        compiler_params=PARAMS,
        cost_estimate=pl.CostEstimate(
            flops=0, bytes_accessed=4 * array.size, transcendentals=0
        ),
        name="copied",
    )(array)


def body(activations, out_grad, key_grad, key_weight, plan, first_moment, second_moment):
    assert lax.axis_size("dp") == 4
    acts = activations[0]
    weight = key_weight[0]
    micro, tokens, feats = acts.shape
    columns = weight.shape[1]
    shard_rows = first_moment.shape[2]
    half = shard_rows // 2
    halves = [(0, half), (half, half)]
    head_pieces, tail_pieces, outward_pieces = halves, halves, halves
    if shard_rows % 1024 == 0:
        eighth = shard_rows // 8
        head_pieces = [(0, 2 * eighth), (2 * eighth, 3 * eighth), (5 * eighth, 3 * eighth)]
        tail_pieces = [(0, 4 * eighth), (4 * eighth, 3 * eighth), (7 * eighth, eighth)]
        outward_pieces = head_pieces
    far_pieces = {3: head_pieces, 2: halves, 1: tail_pieces}
    across_pieces = {0: head_pieces, 1: tail_pieces}
    where_am_i = lax.axis_index("dp")[None]

    def all_heads(keys, before=None):
        count = lax.axis_size("head")
        if count != 2:
            return lax.all_gather(keys, "head", axis=2, tiled=True)
        other = lax.ppermute(keys, "head", [(0, 1), (1, 0)])
        if before is not None:
            other, keys, _ = lax.optimization_barrier((other, keys, before))
        first = lax.axis_index("head") == 0
        return jnp.concatenate(
            [jnp.where(first, keys, other), jnp.where(first, other, keys)], axis=2
        )

    def call(kernel, specs, out_spec, shape, flops, operands, scalar=where_am_i, **more):
        moved = sum(array.size for array in jax.tree.leaves(shape)) * 6
        return pl.pallas_call(
            kernel,
            grid_spec=pltpu.PrefetchScalarGridSpec(
                num_scalar_prefetch=1,
                grid=more.pop("grid", (1,)),
                in_specs=specs,
                out_specs=out_spec,
                scratch_shapes=more.pop("scratch_shapes", ()),
            ),
            out_shape=shape,
            compiler_params=more.pop("params", PARAMS),
            cost_estimate=pl.CostEstimate(
                flops=flops, bytes_accessed=moved, transcendentals=0
            ),
            **more,
        )(scalar, *operands)

    def slices(wanted, params):
        parts = call(
            functools.partial(slice_kernel, shard_rows, wanted),
            [ANYWHERE],
            [IN_VMEM] * len(wanted),
            [
                jax.ShapeDtypeStruct((micro, tokens, size), acts.dtype)
                for _, _, size in wanted
            ],
            0,
            (acts,),
            scratch_shapes=[pltpu.SemaphoreType.DMA((len(wanted),))],
            params=params,
        )
        return {(shard, offset): part for (shard, offset, _), part in zip(wanted, parts)}

    near_keys = key_grad[0]
    far_near_keys = lax.ppermute(near_keys, "dp", INWARD)
    all_keys = all_heads(near_keys)
    wanted = [(shard, *piece) for shard in (3, 2, 1) for piece in far_pieces[shard]]
    outgoing = slices(wanted[:2], CUT_PARAMS) | slices(wanted[2:], PARAMS)
    far_acts = {}
    for shard in (3, 2, 1):
        for offset, size in far_pieces[shard]:
            far_acts[shard, offset] = lax.ppermute(outgoing[shard, offset], "dp", INWARD)
    relay_shape = jax.ShapeDtypeStruct((tokens, feats), jnp.bfloat16)
    relay_flops = 2 * tokens * feats * columns

    def turn_keys(turn):
        return pl.BlockSpec((1, tokens, columns), lambda g, p: (p[turn], 0, 0))

    held_weight = call(
        load_kernel,
        [ANYWHERE],
        IN_VMEM,
        jax.ShapeDtypeStruct(weight.shape, weight.dtype),
        0,
        (weight,),
        scratch_shapes=[pltpu.SemaphoreType.DMA],
        params=LOAD_PARAMS,
    )

    def through(incoming, turn):
        return call(
            functools.partial(relay_kernel, 2),
            [turn_keys(turn), IN_VMEM, IN_VMEM],
            IN_VMEM,
            relay_shape,
            relay_flops,
            (all_keys, incoming, held_weight),
            scalar=plan[0],
        )

    count = lax.axis_size("pipe")
    back = [(source, (source - 1) % count) for source in range(count)]
    passing = through(out_grad[0], 0)
    received = lax.ppermute(passing, "pipe", back)
    passed = copied(lax.ppermute(through(received, 1), "pipe", back))
    far_keys = all_heads(far_near_keys, passing)

    def holder(pieces, offset):
        return max(start for start, _ in pieces if start <= offset)

    def start_of(shard, offset):
        return lambda place: shard_at(place, shard) * shard_rows + offset

    def product(size, terms):
        return 2 * terms * micro * tokens * size * columns

    def pair_sum(shard, offset, size):
        held = holder(far_pieces[shard], offset)
        return call(
            functools.partial(pair_kernel, start_of(shard, offset), offset - held),
            [IN_VMEM] * 4,
            IN_VMEM,
            jax.ShapeDtypeStruct((size, columns), jnp.bfloat16),
            product(size, 2),
            (acts, all_keys, far_acts[shard, held], far_keys),
        )

    def add_own(offset, size, arrived):
        return call(
            functools.partial(add_kernel, start_of(0, offset)),
            [IN_VMEM] * (2 + len(arrived)),
            IN_VMEM,
            jax.ShapeDtypeStruct((size, columns), jnp.bfloat16),
            product(size, 1),
            (acts, all_keys, *arrived),
        )

    across = {}
    for shard in (0, 1):
        for offset, size in across_pieces[shard]:
            total = pair_sum(3 - shard, offset, size)
            across[shard, offset] = lax.ppermute(total, "dp", ACROSS)
    outward = {}
    for offset, size in outward_pieces:
        arrived = [
            across[0, start] for start, _ in head_pieces if offset <= start < offset + size
        ]
        outward[offset] = lax.ppermute(add_own(offset, size, arrived), "dp", OUTWARD)

    split = outward_pieces[-1][0]
    steps = [Update(True, 0, split), Update(True, split, shard_rows - split)]
    inner_steps = [Update(False, *piece) for piece in tail_pieces]
    steps = [steps[0], inner_steps[0], steps[1], *inner_steps[1:]]
    whole = jax.ShapeDtypeStruct((shard_rows, columns), jnp.bfloat16)
    outputs, sums, stash = None, None, None
    for index, step in enumerate(steps):
        offset, size = step.offset, step.size
        last = index == len(steps) - 1
        stashing = index == len(steps) - 2 and not step.at_end
        needed = [
            start
            for start, rows in outward_pieces
            if step.at_end and start < offset + size and offset < start + rows
        ]
        here = where_am_i
        if index == 2:
            here, passed = lax.optimization_barrier((where_am_i, passed))
        operands = [acts, all_keys, held_weight, first_moment[0, 0], second_moment[0, 0]]
        if step.at_end:
            operands += [outward[start] for start in needed]
        else:
            operands += [far_acts[1, offset], far_keys, across[1, offset]]
        operands += [] if sums is None else [sums]
        operands += [] if stash is None else stash[1]
        specs = [IN_VMEM] * len(operands)
        aliases = {}
        if outputs is not None and not stashing:
            aliases = {len(operands) + 1 + which: which for which in range(3)}
            operands += outputs
            specs += [ANYWHERE] * 3
        step = dataclasses.replace(
            step,
            outward_starts=tuple(needed),
            carried=sums is not None,
            stash=stashing,
            stashed=-1 if stash is None else stash[0],
            last=last,
        )
        shape = jax.ShapeDtypeStruct((size, columns), jnp.bfloat16) if stashing else whole
        *rows, sums = call(
            functools.partial(update_kernel, step),
            specs,
            [IN_VMEM if stashing else ANYWHERE] * 3 + [ANYWHERE if last else IN_VMEM],
            [shape] * 3 + [jax.ShapeDtypeStruct((1, columns), jnp.float32)],
            product(size, 2),
            operands,
            scalar=here,
            input_output_aliases=aliases,
            scratch_shapes=[
                pltpu.VMEM((size, columns), jnp.float32),
                pltpu.VMEM((3, size, columns), jnp.bfloat16),
                pltpu.VMEM((1, columns), jnp.float32),
                pltpu.SemaphoreType.DMA((3, size // CHUNK)),
                pltpu.SemaphoreType.DMA((3,)),
                pltpu.SemaphoreType.DMA,
            ],
        )
        if stashing:
            stash = (offset, rows)
        else:
            outputs = rows
    new_weight, new_first, new_second = outputs
    checksum = sums
    return (
        passed[None],
        new_weight[None, None],
        new_first[None, None],
        new_second[None, None],
        checksum[None, None],
    )


def solution(mesh):
    return jax.shard_map(
        body,
        mesh=mesh,
        in_specs=(
            P("pipe", None, "dp", "head"),
            P("pipe", "dp", "head"),
            P("pipe", None, "dp", "head"),
            P("pipe", "head", None),
            P("pipe", None),
            P("pipe", "head", "dp", None),
            P("pipe", "head", "dp", None),
        ),
        out_specs=(
            P("pipe", "dp", "head"),
            P("pipe", "head", "dp", None),
            P("pipe", "head", "dp", None),
            P("pipe", "head", "dp", None),
            P("pipe", "head", "dp", None),
        ),
        check_vma=False,
    )
```

```python
import dataclasses
import functools

import jax
import jax.numpy as jnp
from jax import lax
from jax.experimental import pallas as pl
from jax.experimental.pallas import tpu as pltpu
from jax.sharding import PartitionSpec as P


beta_one = 0.9
beta_two = 0.95
learn_rate = 0.01
weight_decay = 0.1
epsilon = 1e-08
first_fix = 1.0 - (0.9**10) ** 10
second_fix = 1.0 - (0.95**10) ** 10


INWARD = [(0, 1), (3, 2)]
ACROSS = [(1, 2), (2, 1)]
OUTWARD = [(1, 0), (2, 3)]
PARAMS = pltpu.CompilerParams(vmem_limit_bytes=24 * 1024 * 1024)
CUT_PARAMS = pltpu.CompilerParams(vmem_limit_bytes=64_000_000)
LOAD_PARAMS = pltpu.CompilerParams(vmem_limit_bytes=52_000_000)
IN_VMEM = pl.BlockSpec(memory_space=pltpu.VMEM)
ANYWHERE = pl.BlockSpec(memory_space=pl.ANY)


def shard_at(place, shard):
    return jnp.where(place >= 2, 3 - shard, shard)


def outer(rows_ref, keys_ref):
    micro, tokens, rows = rows_ref.shape
    columns = keys_ref.shape[2]
    return lax.dot_general(
        rows_ref[...].reshape(micro * tokens, rows),
        keys_ref[...].reshape(micro * tokens, columns),
        (((0,), (0,)), ((), ())),
        preferred_element_type=jnp.float32,
    )


def own_rows(acts_ref, start, size):
    return acts_ref.at[:, :, pl.ds(pl.multiple_of(start, 128), size)]


def pair_kernel(start_of, far_start, at_ref, acts_ref, keys_ref, far_acts_ref, far_keys_ref, out_ref):
    size = out_ref.shape[0]
    acts = own_rows(acts_ref, start_of(at_ref[0]), size)
    far_acts = far_acts_ref.at[:, :, pl.ds(far_start, size)]
    total = outer(acts, keys_ref) + outer(far_acts, far_keys_ref)
    out_ref[...] = total.astype(out_ref.dtype)


def add_kernel(start_of, at_ref, acts_ref, keys_ref, *refs):
    sum_refs, out_ref = refs[:-1], refs[-1]
    total = outer(own_rows(acts_ref, start_of(at_ref[0]), out_ref.shape[0]), keys_ref)
    start = 0
    for sum_ref in sum_refs:
        rows = sum_ref.shape[0]
        part = total[start : start + rows] + sum_ref[...].astype(jnp.float32)
        out_ref[start : start + rows, :] = part.astype(out_ref.dtype)
        start += rows


@dataclasses.dataclass(frozen=True)
class Update:
    at_end: bool
    offset: int
    size: int
    outward_starts: tuple = ()
    carried: bool = False
    stash: bool = False
    stashed: int = -1
    aliased: int = 0
    ahead: tuple = ()
    ready: bool = False
    closes: bool = False
    last: bool = False
    chunk: int = 128


def update_kernel(
    plan, at_ref, acts_ref, keys_ref, weight_ref, first_ref, second_ref, *refs
):
    taken = len(plan.outward_starts) if plan.at_end else 3
    terms, refs = refs[:taken], list(refs[taken:])
    carried_ref = refs.pop(0) if plan.carried else None
    stashed_refs = [refs.pop(0) for _ in range(3)] if plan.stashed >= 0 else []
    ready_ref = refs.pop(0) if plan.ready else None
    total_ref, staged_ref, sum_ref, sem, old_sem, sum_sem = refs[-6:]
    outs = list(refs[plan.aliased : -6])
    out_refs = [outs.pop(0) for _ in range(3)]
    checksum_ref = outs.pop(0) if plan.closes else None
    column_ref = None if plan.last else outs.pop(0)
    ahead_ref = outs.pop(0) if plan.ahead else None
    chunk = plan.chunk
    shard_rows = first_ref.shape[0]
    offset, size = plan.offset, plan.size
    place = at_ref[0]
    own = place * shard_rows + offset
    is_end = (place == 0) | (place == 3)
    mine = is_end if plan.at_end else jnp.logical_not(is_end)

    def old_copies():
        return [
            pltpu.make_async_copy(
                ref,
                out_refs[which].at[pl.ds(plan.stashed, ref.shape[0])],
                old_sem.at[which],
            )
            for which, ref in enumerate(stashed_refs)
        ]

    def new_copies(row):
        return [
            pltpu.make_async_copy(
                staged_ref.at[which, pl.ds(row, chunk)],
                out_refs[which].at[pl.ds(offset + row, chunk)],
                sem.at[which, row // chunk],
            )
            for which in range(3)
        ]

    sum_ref[...] = carried_ref[...] if plan.carried else jnp.zeros_like(sum_ref)

    @pl.when(mine)
    def _():
        for copy in old_copies():
            copy.start()
        product = ready_ref[...] if plan.ready else outer(own_rows(acts_ref, own, size), keys_ref)
        if not plan.at_end:
            product = product + outer(terms[0], terms[1])
        total_ref[...] = product
        copies = old_copies()
        for row in range(0, size, chunk):
            here = pl.ds(row, chunk)
            there = pl.ds(offset + row, chunk)
            if plan.at_end:
                starts = plan.outward_starts
                piece = max(n for n, start in enumerate(starts) if start <= offset + row)
                arrived = terms[piece][pl.ds(offset + row - starts[piece], chunk), :]
            else:
                arrived = terms[2][here, :]
            gradient = total_ref[here, :] + arrived.astype(jnp.float32)
            sum_ref[...] += jnp.sum(gradient, axis=0, keepdims=True)
            weight_rows = pl.ds(pl.multiple_of(own + row, chunk), chunk)
            old_weight = weight_ref[weight_rows, :].astype(jnp.float32)
            first_fresh = (
                beta_one * first_ref[there, :].astype(jnp.float32) + (1.0 - beta_one) * gradient
            )
            second_fresh = (
                beta_two * second_ref[there, :].astype(jnp.float32)
                + (1.0 - beta_two) * gradient * gradient
            )
            fixed = second_fresh * (1.0 / second_fix)
            step = first_fresh * (learn_rate / first_fix) / (fixed * lax.rsqrt(fixed) + epsilon)
            new_weight = old_weight * (1.0 - learn_rate * weight_decay) - step
            for which, value in enumerate((new_weight, first_fresh, second_fresh)):
                value = value.astype(staged_ref.dtype)
                if plan.stash:
                    out_refs[which][here, :] = value
                else:
                    staged_ref[which, here, :] = value
            if not plan.stash:
                for copy in new_copies(row):
                    copy.start()
                    copies.append(copy)
        if plan.closes:
            sum_ref[...] = sum_ref[...] * (1.0 / shard_rows)
            copies.append(pltpu.make_async_copy(sum_ref, checksum_ref, sum_sem))
            copies[-1].start()
        if plan.ahead:
            start, rows = plan.ahead
            ahead_ref[...] = outer(own_rows(acts_ref, own - offset + start, rows), keys_ref)
        for copy in copies:
            copy.wait()

    if not plan.last:
        column_ref[...] = sum_ref[...]


def slice_kernel(rows_in_shard, wanted, at_ref, acts_ref, *refs):
    outs, sem = refs[: len(wanted)], refs[len(wanted)]
    copies = []
    for index, (shard, offset, size) in enumerate(wanted):
        start = pl.multiple_of(shard_at(at_ref[0], shard) * rows_in_shard + offset, 128)
        copies.append(
            pltpu.make_async_copy(
                acts_ref.at[:, :, pl.ds(start, size)], outs[index], sem.at[index]
            )
        )
    for copy in copies:
        copy.start()
    for copy in copies:
        copy.wait()


def relay_kernel(parts, plan_ref, keys_ref, incoming_ref, weight_ref, out_ref):
    width = weight_ref.shape[0] // parts
    for index in range(parts):
        part = pl.ds(index * width, width)
        added = lax.dot_general(
            keys_ref[0],
            weight_ref[part, :],
            (((1,), (1,)), ((), ())),
            preferred_element_type=jnp.float32,
        )
        total = incoming_ref[:, part].astype(jnp.float32) + added
        out_ref[:, part] = total.astype(out_ref.dtype)


def load_kernel(at_ref, source_ref, target_ref, sem):
    copy = pltpu.make_async_copy(source_ref, target_ref, sem)
    copy.start()
    copy.wait()


def copy_kernel(pieces, source_ref, target_ref, buffer, in_sem, out_sem):
    rows = source_ref.shape[0] // pieces
    ins, outs = [], []
    for index in range(pieces):
        part = pl.ds(index * rows, rows)
        ins.append(
            pltpu.make_async_copy(source_ref.at[part], buffer.at[part], in_sem.at[index])
        )
        outs.append(
            pltpu.make_async_copy(buffer.at[part], target_ref.at[part], out_sem.at[index])
        )
    for copy in ins:
        copy.start()
    for arriving, leaving in zip(ins, outs):
        arriving.wait()
        leaving.start()
    for copy in outs:
        copy.wait()


def copied(array):
    pieces = 7 if array.shape[0] % (7 * 16) == 0 else 1
    return pl.pallas_call(
        functools.partial(copy_kernel, pieces),
        in_specs=[ANYWHERE],
        out_specs=ANYWHERE,
        out_shape=jax.ShapeDtypeStruct(array.shape, array.dtype),
        scratch_shapes=[
            pltpu.VMEM(array.shape, array.dtype),
            pltpu.SemaphoreType.DMA((pieces,)),
            pltpu.SemaphoreType.DMA((pieces,)),
        ],
        compiler_params=PARAMS,
        cost_estimate=pl.CostEstimate(
            flops=0, bytes_accessed=4 * array.size, transcendentals=0
        ),
        name="copied",
    )(array)


def body(activations, out_grad, key_grad, key_weight, plan, first_moment, second_moment):
    assert lax.axis_size("dp") == 4
    acts = activations[0]
    weight = key_weight[0]
    micro, tokens, feats = acts.shape
    columns = weight.shape[1]
    shard_rows = first_moment.shape[2]
    half = shard_rows // 2
    halves = [(0, half), (half, half)]
    head_pieces, tail_pieces, outward_pieces = halves, halves, halves
    if shard_rows % 1024 == 0:
        eighth = shard_rows // 8
        head_pieces = [(0, 2 * eighth), (2 * eighth, 3 * eighth), (5 * eighth, 3 * eighth)]
        tail_pieces = [(0, 4 * eighth), (4 * eighth, 3 * eighth), (7 * eighth, eighth)]
        outward_pieces = head_pieces
    far_pieces = {3: head_pieces, 2: halves, 1: tail_pieces}
    across_pieces = {0: head_pieces, 1: tail_pieces}
    where_am_i = lax.axis_index("dp")[None]

    def all_heads(keys, before=None):
        count = lax.axis_size("head")
        if count != 2:
            return lax.all_gather(keys, "head", axis=2, tiled=True)
        other = lax.ppermute(keys, "head", [(0, 1), (1, 0)])
        if before is not None:
            other, keys, _ = lax.optimization_barrier((other, keys, before))
        first = lax.axis_index("head") == 0
        return jnp.concatenate(
            [jnp.where(first, keys, other), jnp.where(first, other, keys)], axis=2
        )

    def call(kernel, specs, out_spec, shape, flops, operands, scalar=where_am_i, **more):
        moved = sum(array.size for array in jax.tree.leaves(shape)) * 6
        return pl.pallas_call(
            kernel,
            grid_spec=pltpu.PrefetchScalarGridSpec(
                num_scalar_prefetch=1,
                grid=more.pop("grid", (1,)),
                in_specs=specs,
                out_specs=out_spec,
                scratch_shapes=more.pop("scratch_shapes", ()),
            ),
            out_shape=shape,
            compiler_params=more.pop("params", PARAMS),
            cost_estimate=pl.CostEstimate(
                flops=flops, bytes_accessed=moved, transcendentals=0
            ),
            **more,
        )(scalar, *operands)

    def slices(wanted, params):
        parts = call(
            functools.partial(slice_kernel, shard_rows, wanted),
            [ANYWHERE],
            [IN_VMEM] * len(wanted),
            [
                jax.ShapeDtypeStruct((micro, tokens, size), acts.dtype)
                for _, _, size in wanted
            ],
            0,
            (acts,),
            scratch_shapes=[pltpu.SemaphoreType.DMA((len(wanted),))],
            params=params,
        )
        return {(shard, offset): part for (shard, offset, _), part in zip(wanted, parts)}

    near_keys = key_grad[0]
    far_near_keys = lax.ppermute(near_keys, "dp", INWARD)
    all_keys = all_heads(near_keys)
    wanted = [(shard, *piece) for shard in (3, 2, 1) for piece in far_pieces[shard]]
    outgoing = slices(wanted[:2], CUT_PARAMS) | slices(wanted[2:], PARAMS)
    far_acts = {}
    for shard in (3, 2, 1):
        for offset, size in far_pieces[shard]:
            far_acts[shard, offset] = lax.ppermute(outgoing[shard, offset], "dp", INWARD)
    relay_shape = jax.ShapeDtypeStruct((tokens, feats), jnp.bfloat16)
    relay_flops = 2 * tokens * feats * columns

    def turn_keys(turn):
        return pl.BlockSpec((1, tokens, columns), lambda g, p: (p[turn], 0, 0))

    held_weight = call(
        load_kernel,
        [ANYWHERE],
        IN_VMEM,
        jax.ShapeDtypeStruct(weight.shape, weight.dtype),
        0,
        (weight,),
        scratch_shapes=[pltpu.SemaphoreType.DMA],
        params=LOAD_PARAMS,
    )

    def through(incoming, turn):
        return call(
            functools.partial(relay_kernel, 2),
            [turn_keys(turn), IN_VMEM, IN_VMEM],
            IN_VMEM,
            relay_shape,
            relay_flops,
            (all_keys, incoming, held_weight),
            scalar=plan[0],
        )

    count = lax.axis_size("pipe")
    back = [(source, (source - 1) % count) for source in range(count)]
    passing = through(out_grad[0], 0)
    received = lax.ppermute(passing, "pipe", back)
    passed = copied(lax.ppermute(through(received, 1), "pipe", back))
    far_keys = all_heads(far_near_keys, passing)

    def holder(pieces, offset):
        return max(start for start, _ in pieces if start <= offset)

    def start_of(shard, offset):
        return lambda place: shard_at(place, shard) * shard_rows + offset

    def product(size, terms):
        return 2 * terms * micro * tokens * size * columns

    def pair_sum(shard, offset, size):
        held = holder(far_pieces[shard], offset)
        return call(
            functools.partial(pair_kernel, start_of(shard, offset), offset - held),
            [IN_VMEM] * 4,
            IN_VMEM,
            jax.ShapeDtypeStruct((size, columns), jnp.bfloat16),
            product(size, 2),
            (acts, all_keys, far_acts[shard, held], far_keys),
        )

    def add_own(offset, size, arrived):
        return call(
            functools.partial(add_kernel, start_of(0, offset)),
            [IN_VMEM] * (2 + len(arrived)),
            IN_VMEM,
            jax.ShapeDtypeStruct((size, columns), jnp.bfloat16),
            product(size, 1),
            (acts, all_keys, *arrived),
        )

    across = {}
    for shard in (0, 1):
        for offset, size in across_pieces[shard]:
            total = pair_sum(3 - shard, offset, size)
            across[shard, offset] = lax.ppermute(total, "dp", ACROSS)
    outward = {}
    for offset, size in outward_pieces:
        arrived = [
            across[0, start] for start, _ in head_pieces if offset <= start < offset + size
        ]
        outward[offset] = lax.ppermute(add_own(offset, size, arrived), "dp", OUTWARD)

    split = outward_pieces[-1][0]
    end_steps = [Update(True, 0, split), Update(True, split, shard_rows - split, closes=True)]
    inner_steps = [Update(False, *piece) for piece in tail_pieces]
    inner_steps[-1] = dataclasses.replace(inner_steps[-1], closes=True, last=True)
    steps = [end_steps[0], inner_steps[0], end_steps[1], *inner_steps[1:]]
    whole = jax.ShapeDtypeStruct((shard_rows, columns), jnp.bfloat16)
    column_shape = jax.ShapeDtypeStruct((1, columns), jnp.float32)
    outputs, checksum, sums, stash = [], [], [], []
    for index, step in enumerate(steps):
        offset, size = step.offset, step.size
        stashing = index == len(steps) - 2 and not step.at_end
        needed = [
            start
            for start, rows in outward_pieces
            if step.at_end and start < offset + size and offset < start + rows
        ]
        here = where_am_i
        if index == 2:
            here, passed = lax.optimization_barrier((where_am_i, passed))
        operands = [acts, all_keys, held_weight, first_moment[0, 0], second_moment[0, 0]]
        if step.at_end:
            operands += [outward[start] for start in needed]
        else:
            operands += [far_acts[1, offset], far_keys, across[1, offset]]
        operands += sums + stash
        written = [] if stashing else outputs + (checksum if step.last else [])
        step = dataclasses.replace(
            step,
            outward_starts=tuple(needed),
            carried=bool(sums),
            stash=stashing,
            stashed=steps[index - 1].offset if stash else -1,
            aliased=len(written),
            ahead=(steps[-1].offset, steps[-1].size) if stashing else (),
            ready=bool(stash),
        )
        specs = [IN_VMEM] * len(operands) + [ANYWHERE] * len(written)
        aliases = {len(operands) + 1 + which: which for which in range(len(written))}
        operands += written
        row_shape = jax.ShapeDtypeStruct((size, columns), jnp.bfloat16) if stashing else whole
        shapes = [row_shape] * 3
        out_specs = [IN_VMEM if stashing else ANYWHERE] * 3
        if step.closes:
            shapes.append(column_shape)
            out_specs.append(ANYWHERE)
        if not step.last:
            shapes.append(column_shape)
            out_specs.append(IN_VMEM)
        if step.ahead:
            shapes.append(jax.ShapeDtypeStruct((step.ahead[1], columns), jnp.float32))
            out_specs.append(IN_VMEM)
        results = call(
            functools.partial(update_kernel, step),
            specs,
            out_specs,
            shapes,
            product(size, 2),
            operands,
            scalar=here,
            input_output_aliases=aliases,
            scratch_shapes=[
                pltpu.VMEM((size, columns), jnp.float32),
                pltpu.VMEM((3, size, columns), jnp.bfloat16),
                pltpu.VMEM((1, columns), jnp.float32),
                pltpu.SemaphoreType.DMA((3, size // step.chunk)),
                pltpu.SemaphoreType.DMA((3,)),
                pltpu.SemaphoreType.DMA,
            ],
        )
        rows, rest = list(results[:3]), list(results[3:])
        if step.closes:
            checksum = [rest.pop(0)]
        if not step.last:
            sums = [rest.pop(0)]
        if stashing:
            stash = rows + rest
        else:
            outputs = rows
    new_weight, new_first, new_second = outputs
    (checksum,) = checksum
    return (
        passed[None],
        new_weight[None, None],
        new_first[None, None],
        new_second[None, None],
        checksum[None, None],
    )


def solution(mesh):
    return jax.shard_map(
        body,
        mesh=mesh,
        in_specs=(
            P("pipe", None, "dp", "head"),
            P("pipe", "dp", "head"),
            P("pipe", None, "dp", "head"),
            P("pipe", "head", None),
            P("pipe", None),
            P("pipe", "head", "dp", None),
            P("pipe", "head", "dp", None),
        ),
        out_specs=(
            P("pipe", "dp", "head"),
            P("pipe", "head", "dp", None),
            P("pipe", "head", "dp", None),
            P("pipe", "head", "dp", None),
            P("pipe", "head", "dp", None),
        ),
        check_vma=False,
    )
```

```python
import dataclasses
import functools

import jax
import jax.numpy as jnp
from jax import lax
from jax.experimental import pallas as pl
from jax.experimental.pallas import tpu as pltpu
from jax.sharding import PartitionSpec as P


beta_one = 0.9
beta_two = 0.95
learn_rate = 0.01
weight_decay = 0.1
epsilon = 1e-08
first_fix = 1.0 - (0.9**10) ** 10
second_fix = 1.0 - (0.95**10) ** 10


INWARD = [(0, 1), (3, 2)]
ACROSS = [(1, 2), (2, 1)]
OUTWARD = [(1, 0), (2, 3)]
PARAMS = pltpu.CompilerParams(vmem_limit_bytes=24 * 1024 * 1024)
CUT_PARAMS = pltpu.CompilerParams(vmem_limit_bytes=54_000_000)
LOAD_PARAMS = pltpu.CompilerParams(vmem_limit_bytes=52_000_000)
IN_VMEM = pl.BlockSpec(memory_space=pltpu.VMEM)
ANYWHERE = pl.BlockSpec(memory_space=pl.ANY)


def shard_at(place, shard):
    return jnp.where(place >= 2, 3 - shard, shard)


def outer(rows_ref, keys_ref):
    micro, tokens, rows = rows_ref.shape
    columns = keys_ref.shape[2]
    return lax.dot_general(
        rows_ref[...].reshape(micro * tokens, rows),
        keys_ref[...].reshape(micro * tokens, columns),
        (((0,), (0,)), ((), ())),
        preferred_element_type=jnp.float32,
    )


def own_rows(acts_ref, start, size):
    return acts_ref.at[:, :, pl.ds(pl.multiple_of(start, 128), size)]


def pair_kernel(start_of, far_start, at_ref, acts_ref, keys_ref, far_acts_ref, far_keys_ref, out_ref):
    size = out_ref.shape[0]
    acts = own_rows(acts_ref, start_of(at_ref[0]), size)
    far_acts = far_acts_ref.at[:, :, pl.ds(far_start, size)]
    total = outer(acts, keys_ref) + outer(far_acts, far_keys_ref)
    out_ref[...] = total.astype(out_ref.dtype)


def add_kernel(start_of, at_ref, acts_ref, keys_ref, *refs):
    sum_refs, out_ref = refs[:-1], refs[-1]
    total = outer(own_rows(acts_ref, start_of(at_ref[0]), out_ref.shape[0]), keys_ref)
    start = 0
    for sum_ref in sum_refs:
        rows = sum_ref.shape[0]
        part = total[start : start + rows] + sum_ref[...].astype(jnp.float32)
        out_ref[start : start + rows, :] = part.astype(out_ref.dtype)
        start += rows


@dataclasses.dataclass(frozen=True)
class Update:
    at_end: bool
    offset: int
    size: int
    outward_starts: tuple = ()
    carried: bool = False
    stash: bool = False
    stashed: int = -1
    aliased: int = 0
    ahead: tuple = ()
    ready: int = -1
    closes: bool = False
    last: bool = False
    chunk: int = 128


def update_kernel(
    plan, at_ref, acts_ref, keys_ref, weight_ref, first_ref, second_ref, *refs
):
    taken = len(plan.outward_starts) if plan.at_end else 3
    terms, refs = refs[:taken], list(refs[taken:])
    carried_ref = refs.pop(0) if plan.carried else None
    stashed_refs = [refs.pop(0) for _ in range(3)] if plan.stashed >= 0 else []
    ready_ref = refs.pop(0) if plan.ready >= 0 else None
    total_ref, staged_ref, sum_ref, sem, old_sem, sum_sem = refs[-6:]
    outs = list(refs[plan.aliased : -6])
    out_refs = [outs.pop(0) for _ in range(3)]
    checksum_ref = outs.pop(0) if plan.closes else None
    column_ref = None if plan.last else outs.pop(0)
    ahead_ref = outs.pop(0) if plan.ahead else None
    chunk = plan.chunk
    shard_rows = first_ref.shape[0]
    offset, size = plan.offset, plan.size
    place = at_ref[0]
    own = place * shard_rows + offset
    is_end = (place == 0) | (place == 3)
    mine = is_end if plan.at_end else jnp.logical_not(is_end)

    def old_copies():
        return [
            pltpu.make_async_copy(
                ref,
                out_refs[which].at[pl.ds(plan.stashed, ref.shape[0])],
                old_sem.at[which],
            )
            for which, ref in enumerate(stashed_refs)
        ]

    def new_copies(row):
        return [
            pltpu.make_async_copy(
                staged_ref.at[which, pl.ds(row, chunk)],
                out_refs[which].at[pl.ds(offset + row, chunk)],
                sem.at[which, row // chunk],
            )
            for which in range(3)
        ]

    sum_ref[...] = carried_ref[...] if plan.carried else jnp.zeros_like(sum_ref)

    @pl.when(mine)
    def _():
        for copy in old_copies():
            copy.start()
        if plan.ready >= 0:
            product = ready_ref[offset - plan.ready : offset - plan.ready + size, :]
        else:
            product = outer(own_rows(acts_ref, own, size), keys_ref)
        if not plan.at_end:
            product = product + outer(terms[0], terms[1])
        total_ref[...] = product
        copies = old_copies()
        for row in range(0, size, chunk):
            here = pl.ds(row, chunk)
            there = pl.ds(offset + row, chunk)
            if plan.at_end:
                starts = plan.outward_starts
                piece = max(n for n, start in enumerate(starts) if start <= offset + row)
                arrived = terms[piece][pl.ds(offset + row - starts[piece], chunk), :]
            else:
                arrived = terms[2][here, :]
            gradient = total_ref[here, :] + arrived.astype(jnp.float32)
            sum_ref[...] += jnp.sum(gradient, axis=0, keepdims=True)
            if plan.closes and row + chunk == size:
                sum_ref[...] = sum_ref[...] * (1.0 / shard_rows)
                copies.append(pltpu.make_async_copy(sum_ref, checksum_ref, sum_sem))
                copies[-1].start()
            weight_rows = pl.ds(pl.multiple_of(own + row, chunk), chunk)
            old_weight = weight_ref[weight_rows, :].astype(jnp.float32)
            first_fresh = (
                beta_one * first_ref[there, :].astype(jnp.float32) + (1.0 - beta_one) * gradient
            )
            second_fresh = (
                beta_two * second_ref[there, :].astype(jnp.float32)
                + (1.0 - beta_two) * gradient * gradient
            )
            fixed = second_fresh * (1.0 / second_fix)
            step = first_fresh * (learn_rate / first_fix) / (fixed * lax.rsqrt(fixed) + epsilon)
            new_weight = old_weight * (1.0 - learn_rate * weight_decay) - step
            for which, value in enumerate((new_weight, first_fresh, second_fresh)):
                value = value.astype(staged_ref.dtype)
                if plan.stash:
                    out_refs[which][here, :] = value
                else:
                    staged_ref[which, here, :] = value
            if not plan.stash:
                for copy in new_copies(row):
                    copy.start()
                    copies.append(copy)
        if plan.ahead:
            start, rows = plan.ahead
            ahead_ref[...] = outer(own_rows(acts_ref, own - offset + start, rows), keys_ref)
        for copy in copies:
            copy.wait()

    if not plan.last:
        column_ref[...] = sum_ref[...]


def slice_kernel(rows_in_shard, wanted, at_ref, acts_ref, *refs):
    outs, sem = refs[: len(wanted)], refs[len(wanted)]
    copies = []
    for index, (shard, offset, size) in enumerate(wanted):
        start = pl.multiple_of(shard_at(at_ref[0], shard) * rows_in_shard + offset, 128)
        copies.append(
            pltpu.make_async_copy(
                acts_ref.at[:, :, pl.ds(start, size)], outs[index], sem.at[index]
            )
        )
    for copy in copies:
        copy.start()
    for copy in copies:
        copy.wait()


def relay_kernel(parts, plan_ref, keys_ref, incoming_ref, weight_ref, out_ref):
    width = weight_ref.shape[0] // parts
    for index in range(parts):
        part = pl.ds(index * width, width)
        added = lax.dot_general(
            keys_ref[0],
            weight_ref[part, :],
            (((1,), (1,)), ((), ())),
            preferred_element_type=jnp.float32,
        )
        total = incoming_ref[:, part].astype(jnp.float32) + added
        out_ref[:, part] = total.astype(out_ref.dtype)


def load_kernel(at_ref, source_ref, target_ref, sem):
    copy = pltpu.make_async_copy(source_ref, target_ref, sem)
    copy.start()
    copy.wait()


def copy_kernel(pieces, source_ref, target_ref, buffer, in_sem, out_sem):
    rows = source_ref.shape[0] // pieces
    ins, outs = [], []
    for index in range(pieces):
        part = pl.ds(index * rows, rows)
        ins.append(
            pltpu.make_async_copy(source_ref.at[part], buffer.at[part], in_sem.at[index])
        )
        outs.append(
            pltpu.make_async_copy(buffer.at[part], target_ref.at[part], out_sem.at[index])
        )
    for copy in ins:
        copy.start()
    for arriving, leaving in zip(ins, outs):
        arriving.wait()
        leaving.start()
    for copy in outs:
        copy.wait()


def copied(array):
    pieces = 7 if array.shape[0] % (7 * 16) == 0 else 1
    return pl.pallas_call(
        functools.partial(copy_kernel, pieces),
        in_specs=[ANYWHERE],
        out_specs=ANYWHERE,
        out_shape=jax.ShapeDtypeStruct(array.shape, array.dtype),
        scratch_shapes=[
            pltpu.VMEM(array.shape, array.dtype),
            pltpu.SemaphoreType.DMA((pieces,)),
            pltpu.SemaphoreType.DMA((pieces,)),
        ],
        compiler_params=PARAMS,
        cost_estimate=pl.CostEstimate(
            flops=0, bytes_accessed=4 * array.size, transcendentals=0
        ),
        name="copied",
    )(array)


def body(activations, out_grad, key_grad, key_weight, plan, first_moment, second_moment):
    assert lax.axis_size("dp") == 4
    acts = activations[0]
    weight = key_weight[0]
    micro, tokens, feats = acts.shape
    columns = weight.shape[1]
    shard_rows = first_moment.shape[2]
    half = shard_rows // 2
    halves = [(0, half), (half, half)]
    head_pieces, tail_pieces, outward_pieces = halves, halves, halves
    if shard_rows % 1024 == 0:
        eighth = shard_rows // 8
        head_pieces = [(0, 2 * eighth), (2 * eighth, 3 * eighth), (5 * eighth, 3 * eighth)]
        tail_pieces = [(0, 4 * eighth), (4 * eighth, 2 * eighth)]
        tail_pieces += [(6 * eighth, eighth), (7 * eighth, eighth)]
        outward_pieces = head_pieces
    far_pieces = {3: head_pieces, 2: halves, 1: tail_pieces}
    across_pieces = {0: head_pieces, 1: tail_pieces}
    where_am_i = lax.axis_index("dp")[None]

    def all_heads(keys, before=None):
        count = lax.axis_size("head")
        if count != 2:
            return lax.all_gather(keys, "head", axis=2, tiled=True)
        other = lax.ppermute(keys, "head", [(0, 1), (1, 0)])
        if before is not None:
            other, keys, _ = lax.optimization_barrier((other, keys, before))
        first = lax.axis_index("head") == 0
        return jnp.concatenate(
            [jnp.where(first, keys, other), jnp.where(first, other, keys)], axis=2
        )

    def call(kernel, specs, out_spec, shape, flops, operands, scalar=where_am_i, **more):
        moved = sum(array.size for array in jax.tree.leaves(shape)) * 6
        return pl.pallas_call(
            kernel,
            grid_spec=pltpu.PrefetchScalarGridSpec(
                num_scalar_prefetch=1,
                grid=more.pop("grid", (1,)),
                in_specs=specs,
                out_specs=out_spec,
                scratch_shapes=more.pop("scratch_shapes", ()),
            ),
            out_shape=shape,
            compiler_params=more.pop("params", PARAMS),
            cost_estimate=pl.CostEstimate(
                flops=flops, bytes_accessed=moved, transcendentals=0
            ),
            **more,
        )(scalar, *operands)

    def slices(wanted, params):
        parts = call(
            functools.partial(slice_kernel, shard_rows, wanted),
            [ANYWHERE],
            [IN_VMEM] * len(wanted),
            [
                jax.ShapeDtypeStruct((micro, tokens, size), acts.dtype)
                for _, _, size in wanted
            ],
            0,
            (acts,),
            scratch_shapes=[pltpu.SemaphoreType.DMA((len(wanted),))],
            params=params,
        )
        return {(shard, offset): part for (shard, offset, _), part in zip(wanted, parts)}

    near_keys = key_grad[0]
    far_near_keys = lax.ppermute(near_keys, "dp", INWARD)
    all_keys = all_heads(near_keys)
    wanted = [(shard, *piece) for shard in (3, 2, 1) for piece in far_pieces[shard]]
    outgoing = slices(wanted[:2], CUT_PARAMS) | slices(wanted[2:], PARAMS)
    far_acts = {}
    for shard in (3, 2, 1):
        for offset, size in far_pieces[shard]:
            far_acts[shard, offset] = lax.ppermute(outgoing[shard, offset], "dp", INWARD)
    relay_shape = jax.ShapeDtypeStruct((tokens, feats), jnp.bfloat16)
    relay_flops = 2 * tokens * feats * columns

    def turn_keys(turn):
        return pl.BlockSpec((1, tokens, columns), lambda g, p: (p[turn], 0, 0))

    held_weight = call(
        load_kernel,
        [ANYWHERE],
        IN_VMEM,
        jax.ShapeDtypeStruct(weight.shape, weight.dtype),
        0,
        (weight,),
        scratch_shapes=[pltpu.SemaphoreType.DMA],
        params=LOAD_PARAMS,
    )

    def through(incoming, turn):
        return call(
            functools.partial(relay_kernel, 2),
            [turn_keys(turn), IN_VMEM, IN_VMEM],
            IN_VMEM,
            relay_shape,
            relay_flops,
            (all_keys, incoming, held_weight),
            scalar=plan[0],
        )

    count = lax.axis_size("pipe")
    back = [(source, (source - 1) % count) for source in range(count)]
    passing = through(out_grad[0], 0)
    received = lax.ppermute(passing, "pipe", back)
    passed = copied(lax.ppermute(through(received, 1), "pipe", back))
    far_keys = all_heads(far_near_keys, passing)

    def holder(pieces, offset):
        return max(start for start, _ in pieces if start <= offset)

    def start_of(shard, offset):
        return lambda place: shard_at(place, shard) * shard_rows + offset

    def product(size, terms):
        return 2 * terms * micro * tokens * size * columns

    def pair_sum(shard, offset, size):
        held = holder(far_pieces[shard], offset)
        return call(
            functools.partial(pair_kernel, start_of(shard, offset), offset - held),
            [IN_VMEM] * 4,
            IN_VMEM,
            jax.ShapeDtypeStruct((size, columns), jnp.bfloat16),
            product(size, 2),
            (acts, all_keys, far_acts[shard, held], far_keys),
        )

    def add_own(offset, size, arrived):
        return call(
            functools.partial(add_kernel, start_of(0, offset)),
            [IN_VMEM] * (2 + len(arrived)),
            IN_VMEM,
            jax.ShapeDtypeStruct((size, columns), jnp.bfloat16),
            product(size, 1),
            (acts, all_keys, *arrived),
        )

    across = {}
    for shard in (0, 1):
        for offset, size in across_pieces[shard]:
            total = pair_sum(3 - shard, offset, size)
            across[shard, offset] = lax.ppermute(total, "dp", ACROSS)
    outward = {}
    for offset, size in outward_pieces:
        arrived = [
            across[0, start] for start, _ in head_pieces if offset <= start < offset + size
        ]
        outward[offset] = lax.ppermute(add_own(offset, size, arrived), "dp", OUTWARD)

    split = outward_pieces[-1][0]
    end_steps = [Update(True, 0, split), Update(True, split, shard_rows - split, closes=True)]
    inner_steps = [Update(False, *piece) for piece in tail_pieces]
    inner_steps[-1] = dataclasses.replace(inner_steps[-1], closes=True, last=True)
    steps = [end_steps[0], inner_steps[0], end_steps[1], *inner_steps[1:]]
    whole = jax.ShapeDtypeStruct((shard_rows, columns), jnp.bfloat16)
    column_shape = jax.ShapeDtypeStruct((1, columns), jnp.float32)
    outputs, checksum, sums, stash, ready = [], [], [], [], []
    for index, step in enumerate(steps):
        offset, size = step.offset, step.size
        stashing = index == len(steps) - 2 and not step.at_end
        needed = [
            start
            for start, rows in outward_pieces
            if step.at_end and start < offset + size and offset < start + rows
        ]
        here = where_am_i
        if index == 2:
            here, passed = lax.optimization_barrier((where_am_i, passed))
        operands = [acts, all_keys, held_weight, first_moment[0, 0], second_moment[0, 0]]
        if step.at_end:
            operands += [outward[start] for start in needed]
        else:
            operands += [far_acts[1, offset], far_keys, across[1, offset]]
        operands += sums + stash + ([] if step.at_end else ready)
        written = [] if stashing else outputs + (checksum if step.last else [])
        step = dataclasses.replace(
            step,
            outward_starts=tuple(needed),
            carried=bool(sums),
            stash=stashing,
            stashed=steps[index - 1].offset if stash else -1,
            aliased=len(written),
            ahead=(size, shard_rows - size) if index == 1 else (),
            ready=tail_pieces[1][0] if ready and not step.at_end else -1,
        )
        specs = [IN_VMEM] * len(operands) + [ANYWHERE] * len(written)
        aliases = {len(operands) + 1 + which: which for which in range(len(written))}
        operands += written
        row_shape = jax.ShapeDtypeStruct((size, columns), jnp.bfloat16) if stashing else whole
        shapes = [row_shape] * 3
        out_specs = [IN_VMEM if stashing else ANYWHERE] * 3
        if step.closes:
            shapes.append(column_shape)
            out_specs.append(ANYWHERE)
        if not step.last:
            shapes.append(column_shape)
            out_specs.append(IN_VMEM)
        if step.ahead:
            shapes.append(jax.ShapeDtypeStruct((step.ahead[1], columns), jnp.float32))
            out_specs.append(IN_VMEM)
        results = call(
            functools.partial(update_kernel, step),
            specs,
            out_specs,
            shapes,
            product(size, 2),
            operands,
            scalar=here,
            input_output_aliases=aliases,
            scratch_shapes=[
                pltpu.VMEM((size, columns), jnp.float32),
                pltpu.VMEM((3, size, columns), jnp.bfloat16),
                pltpu.VMEM((1, columns), jnp.float32),
                pltpu.SemaphoreType.DMA((3, size // step.chunk)),
                pltpu.SemaphoreType.DMA((3,)),
                pltpu.SemaphoreType.DMA,
            ],
        )
        rows, rest = list(results[:3]), list(results[3:])
        if step.closes:
            checksum = [rest.pop(0)]
        if not step.last:
            sums = [rest.pop(0)]
        if step.ahead:
            ready = rest
        if stashing:
            stash = rows
        else:
            outputs = rows
    new_weight, new_first, new_second = outputs
    (checksum,) = checksum
    return (
        passed[None],
        new_weight[None, None],
        new_first[None, None],
        new_second[None, None],
        checksum[None, None],
    )


def solution(mesh):
    return jax.shard_map(
        body,
        mesh=mesh,
        in_specs=(
            P("pipe", None, "dp", "head"),
            P("pipe", "dp", "head"),
            P("pipe", None, "dp", "head"),
            P("pipe", "head", None),
            P("pipe", None),
            P("pipe", "head", "dp", None),
            P("pipe", "head", "dp", None),
        ),
        out_specs=(
            P("pipe", "dp", "head"),
            P("pipe", "head", "dp", None),
            P("pipe", "head", "dp", None),
            P("pipe", "head", "dp", None),
            P("pipe", "head", "dp", None),
        ),
        check_vma=False,
    )
```

```python
import dataclasses
import functools

import jax
import jax.numpy as jnp
from jax import lax
from jax.experimental import pallas as pl
from jax.experimental.pallas import tpu as pltpu
from jax.sharding import PartitionSpec as P


beta_one = 0.9
beta_two = 0.95
learn_rate = 0.01
weight_decay = 0.1
epsilon = 1e-08
first_fix = 1.0 - (0.9**10) ** 10
second_fix = 1.0 - (0.95**10) ** 10


INWARD = [(0, 1), (3, 2)]
ACROSS = [(1, 2), (2, 1)]
OUTWARD = [(1, 0), (2, 3)]
PARAMS = pltpu.CompilerParams(vmem_limit_bytes=24 * 1024 * 1024)
CUT_PARAMS = pltpu.CompilerParams(vmem_limit_bytes=64_000_000)
LOAD_PARAMS = pltpu.CompilerParams(vmem_limit_bytes=52_000_000)
IN_VMEM = pl.BlockSpec(memory_space=pltpu.VMEM)
ANYWHERE = pl.BlockSpec(memory_space=pl.ANY)


def shard_at(place, shard):
    return jnp.where(place >= 2, 3 - shard, shard)


def outer(rows_ref, keys_ref):
    micro, tokens, rows = rows_ref.shape
    columns = keys_ref.shape[2]
    return lax.dot_general(
        rows_ref[...].reshape(micro * tokens, rows),
        keys_ref[...].reshape(micro * tokens, columns),
        (((0,), (0,)), ((), ())),
        preferred_element_type=jnp.float32,
    )


def own_rows(acts_ref, start, size):
    return acts_ref.at[:, :, pl.ds(pl.multiple_of(start, 128), size)]


def pair_kernel(start_of, far_start, at_ref, acts_ref, keys_ref, far_acts_ref, far_keys_ref, out_ref):
    size = out_ref.shape[0]
    acts = own_rows(acts_ref, start_of(at_ref[0]), size)
    far_acts = far_acts_ref.at[:, :, pl.ds(far_start, size)]
    total = outer(acts, keys_ref) + outer(far_acts, far_keys_ref)
    out_ref[...] = total.astype(out_ref.dtype)


def add_kernel(start_of, at_ref, acts_ref, keys_ref, *refs):
    sum_refs, out_ref = refs[:-1], refs[-1]
    total = outer(own_rows(acts_ref, start_of(at_ref[0]), out_ref.shape[0]), keys_ref)
    start = 0
    for sum_ref in sum_refs:
        rows = sum_ref.shape[0]
        part = total[start : start + rows] + sum_ref[...].astype(jnp.float32)
        out_ref[start : start + rows, :] = part.astype(out_ref.dtype)
        start += rows


@dataclasses.dataclass(frozen=True)
class Update:
    at_end: bool
    offset: int
    size: int
    outward_starts: tuple = ()
    carried: bool = False
    stash: bool = False
    stashed: int = -1
    aliased: int = 0
    ahead: tuple = ()
    ready: int = -1
    closes: bool = False
    last: bool = False
    chunk: int = 128


def update_kernel(
    plan, at_ref, acts_ref, keys_ref, weight_ref, first_ref, second_ref, *refs
):
    taken = len(plan.outward_starts) if plan.at_end else 3
    terms, refs = refs[:taken], list(refs[taken:])
    carried_ref = refs.pop(0) if plan.carried else None
    stashed_refs = [refs.pop(0) for _ in range(3)] if plan.stashed >= 0 else []
    ready_ref = refs.pop(0) if plan.ready >= 0 else None
    total_ref, staged_ref, sum_ref, sem, old_sem, sum_sem = refs[-6:]
    outs = list(refs[plan.aliased : -6])
    out_refs = [outs.pop(0) for _ in range(3)]
    checksum_ref = outs.pop(0) if plan.closes else None
    column_ref = None if plan.last else outs.pop(0)
    ahead_ref = outs.pop(0) if plan.ahead else None
    chunk = plan.chunk
    shard_rows = first_ref.shape[0]
    offset, size = plan.offset, plan.size
    place = at_ref[0]
    own = place * shard_rows + offset
    is_end = (place == 0) | (place == 3)
    mine = is_end if plan.at_end else jnp.logical_not(is_end)

    def old_copies():
        return [
            pltpu.make_async_copy(
                ref,
                out_refs[which].at[pl.ds(plan.stashed, ref.shape[0])],
                old_sem.at[which],
            )
            for which, ref in enumerate(stashed_refs)
        ]

    def new_copies(row):
        return [
            pltpu.make_async_copy(
                staged_ref.at[which, pl.ds(row, chunk)],
                out_refs[which].at[pl.ds(offset + row, chunk)],
                sem.at[which, row // chunk],
            )
            for which in range(3)
        ]

    sum_ref[...] = carried_ref[...] if plan.carried else jnp.zeros_like(sum_ref)

    @pl.when(mine)
    def _():
        for copy in old_copies():
            copy.start()
        if plan.ready >= 0:
            product = ready_ref[offset - plan.ready : offset - plan.ready + size, :]
        else:
            product = outer(own_rows(acts_ref, own, size), keys_ref)
        if not plan.at_end:
            product = product + outer(terms[0], terms[1])
        if size > chunk:
            total_ref[...] = product
        copies = old_copies()
        for row in range(0, size, chunk):
            here = pl.ds(row, chunk)
            there = pl.ds(offset + row, chunk)
            if plan.at_end:
                starts = plan.outward_starts
                piece = max(n for n, start in enumerate(starts) if start <= offset + row)
                arrived = terms[piece][pl.ds(offset + row - starts[piece], chunk), :]
            else:
                arrived = terms[2][here, :]
            total = total_ref[here, :] if size > chunk else product
            gradient = total + arrived.astype(jnp.float32)
            sum_ref[...] += jnp.sum(gradient, axis=0, keepdims=True)
            if plan.closes and row + chunk == size:
                sum_ref[...] = sum_ref[...] * (1.0 / shard_rows)
                copies.append(pltpu.make_async_copy(sum_ref, checksum_ref, sum_sem))
                copies[-1].start()
            weight_rows = pl.ds(pl.multiple_of(own + row, chunk), chunk)
            old_weight = weight_ref[weight_rows, :].astype(jnp.float32)
            first_fresh = (
                beta_one * first_ref[there, :].astype(jnp.float32) + (1.0 - beta_one) * gradient
            )
            second_fresh = (
                beta_two * second_ref[there, :].astype(jnp.float32)
                + (1.0 - beta_two) * gradient * gradient
            )
            fixed = second_fresh * (1.0 / second_fix)
            step = first_fresh * (learn_rate / first_fix) / (fixed * lax.rsqrt(fixed) + epsilon)
            new_weight = old_weight * (1.0 - learn_rate * weight_decay) - step
            for which, value in enumerate((new_weight, first_fresh, second_fresh)):
                value = value.astype(staged_ref.dtype)
                if plan.stash:
                    out_refs[which][here, :] = value
                else:
                    staged_ref[which, here, :] = value
            if not plan.stash:
                for copy in new_copies(row):
                    copy.start()
                    copies.append(copy)
        if plan.ahead:
            start, rows = plan.ahead
            ahead_ref[...] = outer(own_rows(acts_ref, own - offset + start, rows), keys_ref)
        for copy in copies:
            copy.wait()

    if not plan.last:
        column_ref[...] = sum_ref[...]


def slice_kernel(rows_in_shard, wanted, at_ref, acts_ref, *refs):
    outs, sem = refs[: len(wanted)], refs[len(wanted)]
    copies = []
    for index, (shard, offset, size) in enumerate(wanted):
        start = pl.multiple_of(shard_at(at_ref[0], shard) * rows_in_shard + offset, 128)
        copies.append(
            pltpu.make_async_copy(
                acts_ref.at[:, :, pl.ds(start, size)], outs[index], sem.at[index]
            )
        )
    for copy in copies:
        copy.start()
    for copy in copies:
        copy.wait()


def relay_kernel(parts, plan_ref, keys_ref, incoming_ref, weight_ref, out_ref):
    width = weight_ref.shape[0] // parts
    for index in range(parts):
        part = pl.ds(index * width, width)
        added = lax.dot_general(
            keys_ref[0],
            weight_ref[part, :],
            (((1,), (1,)), ((), ())),
            preferred_element_type=jnp.float32,
        )
        total = incoming_ref[:, part].astype(jnp.float32) + added
        out_ref[:, part] = total.astype(out_ref.dtype)


def load_kernel(at_ref, source_ref, target_ref, sem):
    copy = pltpu.make_async_copy(source_ref, target_ref, sem)
    copy.start()
    copy.wait()


def copy_kernel(pieces, source_ref, target_ref, buffer, in_sem, out_sem):
    rows = source_ref.shape[0] // pieces
    ins, outs = [], []
    for index in range(pieces):
        part = pl.ds(index * rows, rows)
        ins.append(
            pltpu.make_async_copy(source_ref.at[part], buffer.at[part], in_sem.at[index])
        )
        outs.append(
            pltpu.make_async_copy(buffer.at[part], target_ref.at[part], out_sem.at[index])
        )
    for copy in ins:
        copy.start()
    for arriving, leaving in zip(ins, outs):
        arriving.wait()
        leaving.start()
    for copy in outs:
        copy.wait()


def copied(array):
    pieces = 7 if array.shape[0] % (7 * 16) == 0 else 1
    return pl.pallas_call(
        functools.partial(copy_kernel, pieces),
        in_specs=[ANYWHERE],
        out_specs=ANYWHERE,
        out_shape=jax.ShapeDtypeStruct(array.shape, array.dtype),
        scratch_shapes=[
            pltpu.VMEM(array.shape, array.dtype),
            pltpu.SemaphoreType.DMA((pieces,)),
            pltpu.SemaphoreType.DMA((pieces,)),
        ],
        compiler_params=PARAMS,
        cost_estimate=pl.CostEstimate(
            flops=0, bytes_accessed=4 * array.size, transcendentals=0
        ),
        name="copied",
    )(array)


def body(activations, out_grad, key_grad, key_weight, plan, first_moment, second_moment):
    assert lax.axis_size("dp") == 4
    acts = activations[0]
    weight = key_weight[0]
    micro, tokens, feats = acts.shape
    columns = weight.shape[1]
    shard_rows = first_moment.shape[2]
    half = shard_rows // 2
    halves = [(0, half), (half, half)]
    head_pieces, tail_pieces, outward_pieces = halves, halves, halves
    if shard_rows % 1024 == 0:
        eighth = shard_rows // 8
        head_pieces = [(0, 2 * eighth), (2 * eighth, 3 * eighth), (5 * eighth, 3 * eighth)]
        tail_pieces = [(0, 4 * eighth), (4 * eighth, 3 * eighth), (7 * eighth, eighth)]
        outward_pieces = head_pieces
    far_pieces = {3: head_pieces, 2: halves, 1: tail_pieces}
    across_pieces = {0: head_pieces, 1: tail_pieces}
    where_am_i = lax.axis_index("dp")[None]

    def all_heads(keys, before=None):
        count = lax.axis_size("head")
        if count != 2:
            return lax.all_gather(keys, "head", axis=2, tiled=True)
        other = lax.ppermute(keys, "head", [(0, 1), (1, 0)])
        if before is not None:
            other, keys, _ = lax.optimization_barrier((other, keys, before))
        first = lax.axis_index("head") == 0
        return jnp.concatenate(
            [jnp.where(first, keys, other), jnp.where(first, other, keys)], axis=2
        )

    def call(kernel, specs, out_spec, shape, flops, operands, scalar=where_am_i, **more):
        moved = sum(array.size for array in jax.tree.leaves(shape)) * 6
        return pl.pallas_call(
            kernel,
            grid_spec=pltpu.PrefetchScalarGridSpec(
                num_scalar_prefetch=1,
                grid=more.pop("grid", (1,)),
                in_specs=specs,
                out_specs=out_spec,
                scratch_shapes=more.pop("scratch_shapes", ()),
            ),
            out_shape=shape,
            compiler_params=more.pop("params", PARAMS),
            cost_estimate=pl.CostEstimate(
                flops=flops, bytes_accessed=moved, transcendentals=0
            ),
            **more,
        )(scalar, *operands)

    def slices(wanted, params):
        parts = call(
            functools.partial(slice_kernel, shard_rows, wanted),
            [ANYWHERE],
            [IN_VMEM] * len(wanted),
            [
                jax.ShapeDtypeStruct((micro, tokens, size), acts.dtype)
                for _, _, size in wanted
            ],
            0,
            (acts,),
            scratch_shapes=[pltpu.SemaphoreType.DMA((len(wanted),))],
            params=params,
        )
        return {(shard, offset): part for (shard, offset, _), part in zip(wanted, parts)}

    near_keys = key_grad[0]
    far_near_keys = lax.ppermute(near_keys, "dp", INWARD)
    all_keys = all_heads(near_keys)
    wanted = [(shard, *piece) for shard in (3, 2, 1) for piece in far_pieces[shard]]
    outgoing = slices(wanted[:2], CUT_PARAMS) | slices(wanted[2:], PARAMS)
    far_acts = {}
    for shard in (3, 2, 1):
        for offset, size in far_pieces[shard]:
            far_acts[shard, offset] = lax.ppermute(outgoing[shard, offset], "dp", INWARD)
    relay_shape = jax.ShapeDtypeStruct((tokens, feats), jnp.bfloat16)
    relay_flops = 2 * tokens * feats * columns

    def turn_keys(turn):
        return pl.BlockSpec((1, tokens, columns), lambda g, p: (p[turn], 0, 0))

    held_weight = call(
        load_kernel,
        [ANYWHERE],
        IN_VMEM,
        jax.ShapeDtypeStruct(weight.shape, weight.dtype),
        0,
        (weight,),
        scratch_shapes=[pltpu.SemaphoreType.DMA],
        params=LOAD_PARAMS,
    )

    def through(incoming, turn):
        return call(
            functools.partial(relay_kernel, 2),
            [turn_keys(turn), IN_VMEM, IN_VMEM],
            IN_VMEM,
            relay_shape,
            relay_flops,
            (all_keys, incoming, held_weight),
            scalar=plan[0],
        )

    count = lax.axis_size("pipe")
    back = [(source, (source - 1) % count) for source in range(count)]
    passing = through(out_grad[0], 0)
    received = lax.ppermute(passing, "pipe", back)
    passed = copied(lax.ppermute(through(received, 1), "pipe", back))
    far_keys = all_heads(far_near_keys, passing)

    def holder(pieces, offset):
        return max(start for start, _ in pieces if start <= offset)

    def start_of(shard, offset):
        return lambda place: shard_at(place, shard) * shard_rows + offset

    def product(size, terms):
        return 2 * terms * micro * tokens * size * columns

    def pair_sum(shard, offset, size):
        held = holder(far_pieces[shard], offset)
        return call(
            functools.partial(pair_kernel, start_of(shard, offset), offset - held),
            [IN_VMEM] * 4,
            IN_VMEM,
            jax.ShapeDtypeStruct((size, columns), jnp.bfloat16),
            product(size, 2),
            (acts, all_keys, far_acts[shard, held], far_keys),
        )

    def add_own(offset, size, arrived):
        return call(
            functools.partial(add_kernel, start_of(0, offset)),
            [IN_VMEM] * (2 + len(arrived)),
            IN_VMEM,
            jax.ShapeDtypeStruct((size, columns), jnp.bfloat16),
            product(size, 1),
            (acts, all_keys, *arrived),
        )

    across = {}
    for shard in (0, 1):
        for offset, size in across_pieces[shard]:
            total = pair_sum(3 - shard, offset, size)
            across[shard, offset] = lax.ppermute(total, "dp", ACROSS)
    outward = {}
    for offset, size in outward_pieces:
        arrived = [
            across[0, start] for start, _ in head_pieces if offset <= start < offset + size
        ]
        outward[offset] = lax.ppermute(add_own(offset, size, arrived), "dp", OUTWARD)

    split = outward_pieces[-1][0]
    end_steps = [Update(True, 0, split), Update(True, split, shard_rows - split, closes=True)]
    inner_steps = [Update(False, *piece) for piece in tail_pieces]
    inner_steps[-1] = dataclasses.replace(inner_steps[-1], closes=True, last=True)
    steps = [end_steps[0], inner_steps[0], end_steps[1], *inner_steps[1:]]
    whole = jax.ShapeDtypeStruct((shard_rows, columns), jnp.bfloat16)
    column_shape = jax.ShapeDtypeStruct((1, columns), jnp.float32)
    outputs, checksum, sums, stash, ready = [], [], [], [], []
    for index, step in enumerate(steps):
        offset, size = step.offset, step.size
        stashing = index == len(steps) - 2 and not step.at_end
        needed = [
            start
            for start, rows in outward_pieces
            if step.at_end and start < offset + size and offset < start + rows
        ]
        here = where_am_i
        if index == 2:
            here, passed = lax.optimization_barrier((where_am_i, passed))
        operands = [acts, all_keys, held_weight, first_moment[0, 0], second_moment[0, 0]]
        if step.at_end:
            operands += [outward[start] for start in needed]
        else:
            operands += [far_acts[1, offset], far_keys, across[1, offset]]
        operands += sums + stash + ([] if step.at_end else ready)
        written = [] if stashing else outputs + (checksum if step.last else [])
        step = dataclasses.replace(
            step,
            outward_starts=tuple(needed),
            carried=bool(sums),
            stash=stashing,
            stashed=steps[index - 1].offset if stash else -1,
            aliased=len(written),
            ahead=(size, shard_rows - size) if index == 1 else (),
            ready=tail_pieces[1][0] if ready and not step.at_end else -1,
        )
        specs = [IN_VMEM] * len(operands) + [ANYWHERE] * len(written)
        aliases = {len(operands) + 1 + which: which for which in range(len(written))}
        operands += written
        row_shape = jax.ShapeDtypeStruct((size, columns), jnp.bfloat16) if stashing else whole
        shapes = [row_shape] * 3
        out_specs = [IN_VMEM if stashing else ANYWHERE] * 3
        if step.closes:
            shapes.append(column_shape)
            out_specs.append(ANYWHERE)
        if not step.last:
            shapes.append(column_shape)
            out_specs.append(IN_VMEM)
        if step.ahead:
            shapes.append(jax.ShapeDtypeStruct((step.ahead[1], columns), jnp.float32))
            out_specs.append(IN_VMEM)
        results = call(
            functools.partial(update_kernel, step),
            specs,
            out_specs,
            shapes,
            product(size, 2),
            operands,
            scalar=here,
            input_output_aliases=aliases,
            scratch_shapes=[
                pltpu.VMEM((size, columns), jnp.float32),
                pltpu.VMEM((3, size, columns), jnp.bfloat16),
                pltpu.VMEM((1, columns), jnp.float32),
                pltpu.SemaphoreType.DMA((3, size // step.chunk)),
                pltpu.SemaphoreType.DMA((3,)),
                pltpu.SemaphoreType.DMA,
            ],
        )
        rows, rest = list(results[:3]), list(results[3:])
        if step.closes:
            checksum = [rest.pop(0)]
        if not step.last:
            sums = [rest.pop(0)]
        if step.ahead:
            ready = rest
        if stashing:
            stash = rows
        else:
            outputs = rows
    new_weight, new_first, new_second = outputs
    (checksum,) = checksum
    return (
        passed[None],
        new_weight[None, None],
        new_first[None, None],
        new_second[None, None],
        checksum[None, None],
    )


def solution(mesh):
    return jax.shard_map(
        body,
        mesh=mesh,
        in_specs=(
            P("pipe", None, "dp", "head"),
            P("pipe", "dp", "head"),
            P("pipe", None, "dp", "head"),
            P("pipe", "head", None),
            P("pipe", None),
            P("pipe", "head", "dp", None),
            P("pipe", "head", "dp", None),
        ),
        out_specs=(
            P("pipe", "dp", "head"),
            P("pipe", "head", "dp", None),
            P("pipe", "head", "dp", None),
            P("pipe", "head", "dp", None),
            P("pipe", "head", "dp", None),
        ),
        check_vma=False,
    )
```
